256 devices in a mesh: energy: 2 (over core), space: 128 (over z, y, x).
Axes of the slice: x: 4, y: 4, z: 8, core: 2. Of those that a mesh axis runs over, the one named last changes fastest.
Arguments:
- precond: bfloat16 [2, 256, 2, 512, 512], P('energy', 'space'), may hold values from -2 to 2
- coupling: bfloat16 [256, 2, 512, 512], P('space'), may hold values from -0.046875 to 0.046875
- source: float32 [2, 256, 2, 512, 128], P('energy', 'space'), may hold values from -6 to 6
- sigma_ret: float32 [2, 256, 2, 512], P('energy', 'space'), may hold values from -0.4 to 0.4
- occupation: float32 [2, 128], replicated, may hold values from 0.05 to 0.95
- shift_offsets: int32 [2, 4], replicated, may hold values from -1 to 1, as said below
- shift_weights: float32 [2, 4], replicated, may hold values from 0.3 to 3
Outputs:
- sigma_lesser: bfloat16 [2, 256, 2, 512, 512], P('energy', 'space')
- sigma_greater: bfloat16 [2, 256, 2, 512, 512], P('energy', 'space')
The draws below stay inside these ranges and needn't reach their ends.
Inputs may be any that keep to these rules, and one draw needn't show every extreme that they name: `shift_offsets`: in every energy's list one offset is -1 or 1.
All inputs are finite; a program needn't handle non-finite values.
Results may differ from the reference program's by a relative error of at most 0.015.
Values may be sent and summed in bfloat16 or wider, within the bound.
A program may use at most 64 MiB of HBM per device.

```python
import math
import jax
import jax.numpy as jnp
from jax import lax

M = 512
MODES = 128
NSHIFT = 4
SWEEPS = 4
SPAN = 1
NE = 2
NSLAB = 256


def draw_precond(key, part):
    key_noise, key_real, key_imag = jax.random.split(key, 3)
    full_shape = (NE, NSLAB, 2, M, M)
    spread_noise = jax.random.normal(key_noise, full_shape, jnp.float32)
    spread_noise = spread_noise * (0.25 / math.sqrt(M))
    identity = (jnp.arange(M)[:, None] == jnp.arange(M)[None, :]).astype(jnp.float32)
    diagonal_real = jax.random.uniform(key_real, (NE, NSLAB, 1, M, 1), jnp.float32, 0.6, 1.0)
    diagonal_imag = jax.random.uniform(key_imag, (NE, NSLAB, 1, M, 1), jnp.float32, -0.3, -0.05)
    diagonal = jnp.concatenate([diagonal_real, diagonal_imag], axis=2)
    return (spread_noise * (1.0 - identity) + diagonal * identity).astype(jnp.bfloat16)


def draw_shift_offsets(key, part):
    key_offsets, key_sign = jax.random.split(jax.random.fold_in(key, 17))
    drawn = jax.random.randint(key_offsets, (NE, NSHIFT), -SPAN, SPAN + 1, dtype=jnp.int32)
    side_sign = jax.random.randint(key_sign, (NE, 1), 0, 2, dtype=jnp.int32) * 2 - 1
    return jnp.concatenate([side_sign * SPAN, drawn[:, 1:]], axis=1).astype(jnp.int32)


def block_scale(stream_key, extent, pieces, smallest, high):
    gain, own = 1.0, jax.random.fold_in(stream_key, 6)
    for axis_at, parts in pieces:
        draws = jnp.exp(jax.random.uniform(jax.random.fold_in(own, axis_at), (parts,), jnp.float32, smallest / len(pieces), high / len(pieces)))
        gain = gain * jnp.repeat(draws, extent[axis_at] // parts).reshape([-1 if axis == axis_at else 1 for axis in range(len(extent))])
    return gain


def normal_values(rng, shape, width, reach, shards=(), kind=jnp.bfloat16):
    array = width * jax.random.normal(rng, shape, jnp.float32)
    if shards:
        array = array * block_scale(rng, shape, shards, -0.22, 0.18)
    return jnp.clip(array, -reach, reach).astype(kind)


def setup_inputs(seed: int = 0) -> dict:
    splits = jax.random.split(jax.random.key(seed), 8)
    return {
        "precond": draw_precond(jax.random.fold_in(splits[7], 71), 0),
        "coupling": normal_values(splits[1], (NSLAB, 2, M, M), (32 * M) ** -0.5, 0.046875, ((0, 128),)),
        "source": normal_values(splits[2], (NE, NSLAB, 2, M, MODES), 1.0, 6.0, ((0, 2), (1, 128)), jnp.float32),
        "sigma_ret": jnp.clip(jax.random.uniform(splits[3], (NE, NSLAB, 2, M), jnp.float32, -0.4, 0.4) * block_scale(splits[3], (NE, NSLAB, 2, M), ((0, 2), (1, 128)), -0.4, 0.0), -0.4, 0.4),
        "occupation": jnp.clip(jax.random.uniform(splits[4], (NE, MODES), jnp.float32, 0.05, 0.95), 0.05, 0.95),
        "shift_offsets": draw_shift_offsets(jax.random.fold_in(splits[7], 71), 0),
        "shift_weights": jnp.clip(jnp.exp(jax.random.uniform(splits[6], (NE, NSHIFT), jnp.float32, math.log(0.3), math.log(3.0))), 0.3, 3.0),
    }


def round_trip(values):
    return lax.optimization_barrier(values.astype(jnp.bfloat16)).astype(jnp.float32)


def multiply(first_operand, second_operand):
    return jnp.einsum("...mn,...nk->...mk", first_operand.astype(jnp.float32), second_operand.astype(jnp.float32))


def multiply_adjoint(first_operand, second_operand):
    return jnp.einsum("...nm,...nk->...mk", first_operand.astype(jnp.float32), second_operand.astype(jnp.float32))


def complex_product(matrix, states):
    real_part = multiply(matrix[..., 0, :, :], states[..., 0, :, :]) - multiply(matrix[..., 1, :, :], states[..., 1, :, :])
    imag_part = multiply(matrix[..., 0, :, :], states[..., 1, :, :]) + multiply(matrix[..., 1, :, :], states[..., 0, :, :])
    return jnp.stack([real_part, imag_part], axis=-3)


def adjoint_product(matrix, states):
    real_part = multiply_adjoint(matrix[..., 0, :, :], states[..., 0, :, :]) + multiply_adjoint(matrix[..., 1, :, :], states[..., 1, :, :])
    imag_part = multiply_adjoint(matrix[..., 0, :, :], states[..., 1, :, :]) - multiply_adjoint(matrix[..., 1, :, :], states[..., 0, :, :])
    return jnp.stack([real_part, imag_part], axis=-3)


def solve_energy(precond_one, source_one, sigma_one, coupling):
    states = round_trip(complex_product(precond_one, round_trip(source_one)))
    sigma_real = sigma_one[:, 0, :, None]
    sigma_imag = sigma_one[:, 1, :, None]
    for sweep_index in range(1, SWEEPS):
        upper_term = complex_product(coupling[:-1], states[1:])
        upper_term = jnp.concatenate([upper_term, jnp.zeros_like(upper_term[:1])], axis=0)
        lower_term = round_trip(adjoint_product(coupling[:-1], states[:-1]))
        lower_term = jnp.concatenate([jnp.zeros_like(lower_term[:1]), lower_term], axis=0)
        local_real = sigma_real * states[:, 0] - sigma_imag * states[:, 1]
        local_imag = sigma_real * states[:, 1] + sigma_imag * states[:, 0]
        local_term = jnp.stack([local_real, local_imag], axis=1)
        driven = round_trip(source_one + local_term + upper_term + lower_term)
        states = round_trip(complex_product(precond_one, driven))
    return states.astype(jnp.bfloat16)


def reference(precond, coupling, source, sigma_ret, occupation, shift_offsets, shift_weights):
    all_states = lax.map(lambda packed: solve_energy(packed[0], packed[1], packed[2], coupling), (precond, source, sigma_ret))

    def self_energy(energy_index):
        targets = energy_index + shift_offsets[energy_index]
        inside = (targets >= 0) & (targets < NE)
        clipped = jnp.clip(targets, 0, NE - 1).astype(jnp.int32)
        picked = all_states[clipped].astype(jnp.float32)
        occupied = occupation[clipped]
        weights = jnp.where(inside, shift_weights[energy_index], jnp.zeros_like(shift_weights[energy_index])) / MODES

        def block(scale):
            scaled = round_trip(picked * scale[:, None, None, None, :])
            real_part = jnp.einsum("jsmk,jsnk->smn", picked[:, :, 0], scaled[:, :, 0]) + jnp.einsum("jsmk,jsnk->smn", picked[:, :, 1], scaled[:, :, 1])
            imag_part = jnp.einsum("jsmk,jsnk->smn", picked[:, :, 1], scaled[:, :, 0]) - jnp.einsum("jsmk,jsnk->smn", picked[:, :, 0], scaled[:, :, 1])
            return jnp.stack([real_part, imag_part], axis=1).astype(jnp.bfloat16)

        return block(weights[:, None] * occupied), block(weights[:, None] * (1.0 - occupied))

    sigma_lesser, sigma_greater = lax.map(self_energy, jnp.arange(NE, dtype=jnp.int32))
    return (sigma_lesser, sigma_greater)
```

```python
import functools

import jax
import jax.numpy as jnp
from jax import lax
from jax.experimental import pallas as pl
from jax.experimental.pallas import tpu as pltpu
from jax.sharding import PartitionSpec as P

SWEEPS = 4
MESH = pl.DeviceIdType.MESH
F32 = jnp.float32
BF16 = jnp.bfloat16


def dot(a, b):
    return jnp.dot(a, b, preferred_element_type=F32)


def dot_t(a, b):
    return lax.dot_general(a, b, (((0,), (0,)), ((), ())), preferred_element_type=F32)


def cprod(mr, mi, sr, si):
    return dot(mr, sr) - dot(mi, si), dot(mr, si) + dot(mi, sr)


def cprod_adj(mr, mi, sr, si):
    return dot_t(mr, sr) + dot_t(mi, si), dot_t(mr, si) - dot_t(mi, sr)


def solve_kernel(n, pre_ref, cpl_ref, src_ref, sig_ref, out_ref,
                 st, follow, arrive, hand, send_sem, recv_sem):
    me = lax.axis_index("space")
    en = lax.axis_index("energy")
    prev = lax.rem(me + n - 1, n)
    nxt = lax.rem(me + 1, n)

    barrier = pltpu.get_barrier_semaphore()
    for peer in (prev, nxt):
        pl.semaphore_signal(barrier, inc=1, device_id=(en, peer), device_id_type=MESH)
    pl.semaphore_wait(barrier, 2)

    @pl.when(me == n - 1)
    def _():
        follow[...] = jnp.zeros_like(follow)

    @pl.when(me == 0)
    def _():
        arrive[...] = jnp.zeros_like(arrive)

    for s in range(2):
        sr = src_ref[0, s, 0].astype(BF16)
        si = src_ref[0, s, 1].astype(BF16)
        re, im = cprod(pre_ref[0, s, 0], pre_ref[0, s, 1], sr, si)
        st[s, 0] = re.astype(BF16)
        st[s, 1] = im.astype(BF16)

    def local(s):
        xr = st[s, 0].astype(F32)
        xi = st[s, 1].astype(F32)
        gr = sig_ref[0, s, 0]
        gi = sig_ref[0, s, 1]
        return (src_ref[0, s, 0] + (gr * xr - gi * xi),
                src_ref[0, s, 1] + (gr * xi + gi * xr))

    for sweep in range(SWEEPS - 1):
        to_prev = pltpu.make_async_remote_copy(
            src_ref=st.at[0], dst_ref=follow.at[sweep],
            send_sem=send_sem.at[0, sweep], recv_sem=recv_sem.at[0, sweep],
            device_id=(en, prev), device_id_type=MESH)
        to_next = pltpu.make_async_remote_copy(
            src_ref=hand.at[sweep], dst_ref=arrive.at[sweep],
            send_sem=send_sem.at[1, sweep], recv_sem=recv_sem.at[1, sweep],
            device_id=(en, nxt), device_id_type=MESH)

        @pl.when(me > 0)
        def _():
            to_prev.start()

        hr, hi = cprod_adj(cpl_ref[1, 0], cpl_ref[1, 1], st[1, 0], st[1, 1])
        hand[sweep, 0] = hr.astype(BF16)
        hand[sweep, 1] = hi.astype(BF16)

        @pl.when(me < n - 1)
        def _():
            to_next.start()

        lr, li = cprod_adj(cpl_ref[0, 0], cpl_ref[0, 1], st[0, 0], st[0, 1])
        lr = lr.astype(BF16).astype(F32)
        li = li.astype(BF16).astype(F32)
        a1r, a1i = local(1)
        ur, ui = cprod(cpl_ref[0, 0], cpl_ref[0, 1], st[1, 0], st[1, 1])
        a0r, a0i = local(0)
        d0r = a0r + ur
        d0i = a0i + ui

        @pl.when(me < n - 1)
        def _():
            to_prev.wait_recv()

        fr, fi = cprod(cpl_ref[1, 0], cpl_ref[1, 1], follow[sweep, 0], follow[sweep, 1])
        d1r = ((a1r + fr) + lr).astype(BF16)
        d1i = ((a1i + fi) + li).astype(BF16)

        @pl.when(me > 0)
        def _():
            to_next.wait_recv()

        d0r = (d0r + arrive[sweep, 0].astype(F32)).astype(BF16)
        d0i = (d0i + arrive[sweep, 1].astype(F32)).astype(BF16)

        @pl.when(me > 0)
        def _():
            to_prev.wait_send()

        @pl.when(me < n - 1)
        def _():
            to_next.wait_send()

        n0r, n0i = cprod(pre_ref[0, 0, 0], pre_ref[0, 0, 1], d0r, d0i)
        n1r, n1i = cprod(pre_ref[0, 1, 0], pre_ref[0, 1, 1], d1r, d1i)
        st[0, 0] = n0r.astype(BF16)
        st[0, 1] = n0i.astype(BF16)
        st[1, 0] = n1r.astype(BF16)
        st[1, 1] = n1i.astype(BF16)

    out_ref[...] = st[...][None]


def solve(precond, coupling, source, sigma, n):
    shape = source.shape[:-1] + (source.shape[-1],)
    sweeps = SWEEPS - 1
    half = (2,) + source.shape[3:]
    vmem = pl.BlockSpec(memory_space=pltpu.VMEM)
    return pl.pallas_call(
        functools.partial(solve_kernel, n),
        out_shape=jax.ShapeDtypeStruct(shape, BF16),
        in_specs=[vmem] * 4,
        out_specs=vmem,
        scratch_shapes=[
            pltpu.VMEM((2,) + half, BF16),
            pltpu.VMEM((sweeps,) + half, BF16),
            pltpu.VMEM((sweeps,) + half, BF16),
            pltpu.VMEM((sweeps,) + half, BF16),
            pltpu.SemaphoreType.DMA((2, sweeps)),
            pltpu.SemaphoreType.DMA((2, sweeps)),
        ],
        compiler_params=pltpu.CompilerParams(collective_id=0, has_side_effects=True),
    )(precond, coupling, source, sigma)


def self_energy(picked, scale):
    scaled = (picked.astype(F32) * scale).astype(BF16)
    pr, pi = picked[:, 0], picked[:, 1]
    br, bi = scaled[:, 0], scaled[:, 1]
    ein = functools.partial(jnp.einsum, "smk,snk->smn", preferred_element_type=F32)
    real_part = ein(pr, br) + ein(pi, bi)
    imag_part = ein(pi, br) - ein(pr, bi)
    return jnp.stack([real_part, imag_part], axis=1).astype(BF16)[None]


def body(precond, coupling, source, sigma_ret, occupation, shift_offsets, shift_weights):
    n = lax.axis_size("space")
    mode_count = source.shape[-1]
    energy_total = occupation.shape[0]
    sigma = sigma_ret[..., None]
    states = solve(precond, coupling, source, sigma, n)
    own = states[0]
    other = lax.ppermute(own, "energy", [(0, 1), (1, 0)])
    e = lax.axis_index("energy")
    offsets = lax.dynamic_index_in_dim(shift_offsets, e, 0, keepdims=False)
    weights_here = lax.dynamic_index_in_dim(shift_weights, e, 0, keepdims=False)
    targets = e + offsets
    inside = (targets >= 0) & (targets < energy_total)
    weights = jnp.where(inside, weights_here, jnp.zeros_like(weights_here)) / mode_count
    coef_own = jnp.sum(jnp.where(targets == e, weights, 0.0))
    coef_other = jnp.sum(jnp.where(targets == 1 - e, weights, 0.0))
    occ_own = lax.dynamic_index_in_dim(occupation, e, 0, keepdims=False)
    occ_other = lax.dynamic_index_in_dim(occupation, 1 - e, 0, keepdims=False)
    picked = jnp.concatenate([own, other], axis=-1)
    less = jnp.concatenate([coef_own * occ_own, coef_other * occ_other])
    great = jnp.concatenate([coef_own * (1.0 - occ_own), coef_other * (1.0 - occ_other)])
    return self_energy(picked, less), self_energy(picked, great)


def solution(mesh):
    placed = (
        P("energy", "space", None, None, None),
        P("space", None, None, None),
        P("energy", "space", None, None, None),
        P("energy", "space", None, None),
        P(),
        P(),
        P(),
    )
    return jax.shard_map(
        body,
        mesh=mesh,
        in_specs=placed,
        out_specs=(P("energy", "space", None, None, None), P("energy", "space", None, None, None)),
        check_vma=False,
    )
```

```python
import functools

import jax
import jax.numpy as jnp
from jax import lax
from jax.experimental import pallas as pl
from jax.experimental.pallas import tpu as pltpu
from jax.sharding import PartitionSpec as P

SWEEPS = 4
MESH = pl.DeviceIdType.MESH
F32 = jnp.float32
BF16 = jnp.bfloat16


def dot(a, b):
    return jnp.dot(a, b, preferred_element_type=F32)


def solve_kernel(n, pre_hbm, cpl_hbm, src_hbm, sig_ref, out_ref,
                 pre, cpl, src, ct, st, follow, arrive, hand, other,
                 load_sem, send_sem, recv_sem, swap_sem):
    me = lax.axis_index("space")
    en = lax.axis_index("energy")
    prev = lax.rem(me + n - 1, n)
    nxt = lax.rem(me + 1, n)
    mate = 1 - en
    h = src.shape[-1]

    loads = [pltpu.make_async_copy(src_hbm.at[0], src, load_sem.at[0])]
    loads += [pltpu.make_async_copy(pre_hbm.at[0, s], pre.at[s], load_sem.at[1 + s]) for s in range(2)]
    loads += [pltpu.make_async_copy(cpl_hbm.at[s], cpl.at[s], load_sem.at[3 + s]) for s in range(2)]
    for c in loads:
        c.start()

    barrier = pltpu.get_barrier_semaphore()
    for peer in ((en, prev), (en, nxt), (mate, me)):
        pl.semaphore_signal(barrier, inc=1, device_id=peer, device_id_type=MESH)
    pl.semaphore_wait(barrier, 3)

    @pl.when(me == n - 1)
    def _():
        follow[...] = jnp.zeros_like(follow)

    @pl.when(me == 0)
    def _():
        arrive[...] = jnp.zeros_like(arrive)

    def column(s):
        g = jnp.concatenate([sig_ref[0, s], jnp.zeros((6, sig_ref.shape[-1]), F32)], axis=0).T
        return g[:, 0:1], g[:, 1:2]

    sig = [column(s) for s in range(2)]

    def store(ref, re, im):
        ref[...] = jnp.concatenate([re.astype(BF16), im.astype(BF16)], axis=1)

    def cprod(mr, mi, rhs):
        x = dot(mr, rhs)
        y = dot(mi, rhs)
        return x[:, :h] - y[:, h:], x[:, h:] + y[:, :h]

    def cprod_adj(mr, mi, rhs):
        x = dot(mr, rhs)
        y = dot(mi, rhs)
        return x[:, :h] + y[:, h:], x[:, h:] - y[:, :h]

    def local(s):
        x = st[s].astype(F32)
        xr, xi = x[:, :h], x[:, h:]
        gr, gi = sig[s]
        return (src[s, 0] + (gr * xr - gi * xi), src[s, 1] + (gr * xi + gi * xr))

    def sends(sweep):
        to_prev = pltpu.make_async_remote_copy(
            src_ref=st.at[0], dst_ref=follow.at[sweep],
            send_sem=send_sem.at[0, sweep], recv_sem=recv_sem.at[0, sweep],
            device_id=(en, prev), device_id_type=MESH)
        to_next = pltpu.make_async_remote_copy(
            src_ref=hand.at[sweep], dst_ref=arrive.at[sweep],
            send_sem=send_sem.at[1, sweep], recv_sem=recv_sem.at[1, sweep],
            device_id=(en, nxt), device_id_type=MESH)
        return to_prev, to_next

    sweeps = SWEEPS - 1
    copies = [sends(sweep) for sweep in range(sweeps)]

    loads[0].wait()
    for s in range(2):
        loads[1 + s].wait()
        rhs = jnp.concatenate([src[s, 0].astype(BF16), src[s, 1].astype(BF16)], axis=1)
        re, im = cprod(pre[s, 0], pre[s, 1], rhs)
        store(st.at[s], re, im)
        if s == 0:
            @pl.when(me > 0)
            def _():
                copies[0][0].start()

    for s in range(2):
        loads[3 + s].wait()
        for p in range(2):
            ct[s, p] = cpl[s, p].T

    for sweep in range(sweeps):
        to_prev, to_next = copies[sweep]
        hr, hi = cprod_adj(ct[1, 0], ct[1, 1], st[1])
        store(hand.at[sweep], hr, hi)

        @pl.when(me < n - 1)
        def _():
            to_next.start()

        lr, li = cprod_adj(ct[0, 0], ct[0, 1], st[0])
        lr = lr.astype(BF16).astype(F32)
        li = li.astype(BF16).astype(F32)
        a1r, a1i = local(1)
        ur, ui = cprod(cpl[0, 0], cpl[0, 1], st[1])
        a0r, a0i = local(0)

        @pl.when(me > 0)
        def _():
            to_next.wait_recv()

        x = arrive[sweep].astype(F32)
        d0 = jnp.concatenate([((a0r + ur) + x[:, :h]).astype(BF16),
                              ((a0i + ui) + x[:, h:]).astype(BF16)], axis=1)

        @pl.when(me > 0)
        def _():
            to_prev.wait_send()

        n0r, n0i = cprod(pre[0, 0], pre[0, 1], d0)
        store(st.at[0], n0r, n0i)
        if sweep + 1 < sweeps:
            @pl.when(me > 0)
            def _():
                copies[sweep + 1][0].start()

        @pl.when(me < n - 1)
        def _():
            to_prev.wait_recv()

        fr, fi = cprod(cpl[1, 0], cpl[1, 1], follow[sweep])
        d1 = jnp.concatenate([((a1r + fr) + lr).astype(BF16),
                              ((a1i + fi) + li).astype(BF16)], axis=1)
        n1r, n1i = cprod(pre[1, 0], pre[1, 1], d1)
        store(st.at[1], n1r, n1i)

        @pl.when(me < n - 1)
        def _():
            to_next.wait_send()

    swap = pltpu.make_async_remote_copy(
        src_ref=st, dst_ref=other, send_sem=swap_sem.at[0], recv_sem=swap_sem.at[1],
        device_id=(mate, me), device_id_type=MESH)
    swap.start()
    out_ref[0] = st[...]
    swap.wait()
    out_ref[1] = other[...]


def solve(precond, coupling, source, sigma, n):
    m, h = source.shape[-2:]
    sweeps = SWEEPS - 1
    half = (m, 2 * h)
    vmem = pl.BlockSpec(memory_space=pltpu.VMEM)
    anyspace = pl.BlockSpec(memory_space=pl.ANY)
    return pl.pallas_call(
        functools.partial(solve_kernel, n),
        out_shape=jax.ShapeDtypeStruct((2, 2) + half, BF16),
        in_specs=[anyspace, anyspace, anyspace, vmem],
        out_specs=vmem,
        scratch_shapes=[
            pltpu.VMEM(precond.shape[1:], BF16),
            pltpu.VMEM(coupling.shape, BF16),
            pltpu.VMEM(source.shape[1:], F32),
            pltpu.VMEM(coupling.shape, BF16),
            pltpu.VMEM((2,) + half, BF16),
            pltpu.VMEM((sweeps,) + half, BF16),
            pltpu.VMEM((sweeps,) + half, BF16),
            pltpu.VMEM((sweeps,) + half, BF16),
            pltpu.VMEM((2,) + half, BF16),
            pltpu.SemaphoreType.DMA((5,)),
            pltpu.SemaphoreType.DMA((2, sweeps)),
            pltpu.SemaphoreType.DMA((2, sweeps)),
            pltpu.SemaphoreType.DMA((2,)),
        ],
        compiler_params=pltpu.CompilerParams(collective_id=0, has_side_effects=True),
    )(precond, coupling, source, sigma)


def nt_dot(a, b):
    return lax.dot_general(a, b, (((1,), (1,)), ((), ())), preferred_element_type=F32)


def self_kernel(both_ref, scale_ref, less_ref, great_ref):
    h = both_ref.shape[-1] // 2
    for s in range(2):
        own = both_ref[0, s]
        mate = both_ref[1, s]
        a = jnp.concatenate([own, mate], axis=1)
        swapped = jnp.concatenate([own[:, h:], -own[:, :h], mate[:, h:], -mate[:, :h]], axis=1)
        af = a.astype(F32)
        for q, out in enumerate((less_ref, great_ref)):
            b = (af * scale_ref[q]).astype(BF16)
            out[0, s, 0] = nt_dot(a, b).astype(BF16)
            out[0, s, 1] = nt_dot(swapped, b).astype(BF16)


def self_energy(both, scales):
    m = both.shape[2]
    vmem = pl.BlockSpec(memory_space=pltpu.VMEM)
    shape = jax.ShapeDtypeStruct((1, 2, 2, m, m), BF16)
    return pl.pallas_call(
        self_kernel,
        out_shape=(shape, shape),
        in_specs=[vmem, vmem],
        out_specs=(vmem, vmem),
    )(both, scales)


def body(precond, coupling, source, sigma_ret, occupation, shift_offsets, shift_weights):
    n = lax.axis_size("space")
    mode_count = source.shape[-1]
    energy_total = occupation.shape[0]
    both = solve(precond, coupling, source, sigma_ret, n)
    e = lax.axis_index("energy")
    offsets = lax.dynamic_index_in_dim(shift_offsets, e, 0, keepdims=False)
    weights_here = lax.dynamic_index_in_dim(shift_weights, e, 0, keepdims=False)
    targets = e + offsets
    inside = (targets >= 0) & (targets < energy_total)
    weights = jnp.where(inside, weights_here, jnp.zeros_like(weights_here)) / mode_count
    coef_own = jnp.sum(jnp.where(targets == e, weights, 0.0))
    coef_other = jnp.sum(jnp.where(targets == 1 - e, weights, 0.0))
    occ_own = lax.dynamic_index_in_dim(occupation, e, 0, keepdims=False)
    occ_other = lax.dynamic_index_in_dim(occupation, 1 - e, 0, keepdims=False)
    less = jnp.concatenate([coef_own * occ_own] * 2 + [coef_other * occ_other] * 2)
    great = jnp.concatenate([coef_own * (1.0 - occ_own)] * 2 + [coef_other * (1.0 - occ_other)] * 2)
    scales = jnp.stack([less, great])[:, None, :]
    return self_energy(both, scales)


def solution(mesh):
    placed = (
        P("energy", "space", None, None, None),
        P("space", None, None, None),
        P("energy", "space", None, None, None),
        P("energy", "space", None, None),
        P(),
        P(),
        P(),
    )
    return jax.shard_map(
        body,
        mesh=mesh,
        in_specs=placed,
        out_specs=(P("energy", "space", None, None, None), P("energy", "space", None, None, None)),
        check_vma=False,
    )
```

```python
import functools

import jax
import jax.numpy as jnp
from jax import lax
from jax.experimental import pallas as pl
from jax.experimental.pallas import tpu as pltpu
from jax.sharding import PartitionSpec as P

SWEEPS = 4
MESH = pl.DeviceIdType.MESH
F32 = jnp.float32
BF16 = jnp.bfloat16


def dot(a, b):
    return jnp.dot(a, b, preferred_element_type=F32)


def solve_kernel(n, pre_hbm, cpl_hbm, src_hbm, sig_ref, out_ref,
                 pre, cpl, src, ct, st, follow, arrive, hand, other,
                 load_sem, send_sem, recv_sem, swap_sem):
    me = lax.axis_index("space")
    en = lax.axis_index("energy")
    prev = lax.rem(me + n - 1, n)
    nxt = lax.rem(me + 1, n)
    mate = 1 - en
    h = src.shape[-1]

    loads = [pltpu.make_async_copy(src_hbm.at[0], src, load_sem.at[0])]
    loads += [pltpu.make_async_copy(pre_hbm.at[0, s], pre.at[s], load_sem.at[1 + s]) for s in range(2)]
    loads += [pltpu.make_async_copy(cpl_hbm.at[s], cpl.at[s], load_sem.at[3 + s]) for s in range(2)]
    for c in loads:
        c.start()

    barrier = pltpu.get_barrier_semaphore()
    for peer in ((en, prev), (en, nxt), (mate, me)):
        pl.semaphore_signal(barrier, inc=1, device_id=peer, device_id_type=MESH)
    pl.semaphore_wait(barrier, 3)

    @pl.when(me == n - 1)
    def _():
        follow[...] = jnp.zeros_like(follow)

    @pl.when(me == 0)
    def _():
        arrive[...] = jnp.zeros_like(arrive)

    def column(s):
        g = jnp.concatenate([sig_ref[0, s], jnp.zeros((6, sig_ref.shape[-1]), F32)], axis=0).T
        return g[:, 0:1], g[:, 1:2]

    sig = [column(s) for s in range(2)]

    def store(ref, re, im):
        ref[...] = jnp.concatenate([re.astype(BF16), im.astype(BF16)], axis=1)

    def cprod(mr, mi, rhs):
        x = dot(mr, rhs)
        y = dot(mi, rhs)
        return x[:, :h] - y[:, h:], x[:, h:] + y[:, :h]

    def cprod_adj(mr, mi, rhs):
        x = dot(mr, rhs)
        y = dot(mi, rhs)
        return x[:, :h] + y[:, h:], x[:, h:] - y[:, :h]

    def local(s):
        x = st[s].astype(F32)
        xr, xi = x[:, :h], x[:, h:]
        gr, gi = sig[s]
        return (src[s, 0] + (gr * xr - gi * xi), src[s, 1] + (gr * xi + gi * xr))

    def sends(sweep):
        to_prev = pltpu.make_async_remote_copy(
            src_ref=st.at[0], dst_ref=follow.at[sweep],
            send_sem=send_sem.at[0, sweep], recv_sem=recv_sem.at[0, sweep],
            device_id=(en, prev), device_id_type=MESH)
        to_next = pltpu.make_async_remote_copy(
            src_ref=hand.at[sweep], dst_ref=arrive.at[sweep],
            send_sem=send_sem.at[1, sweep], recv_sem=recv_sem.at[1, sweep],
            device_id=(en, nxt), device_id_type=MESH)
        return to_prev, to_next

    sweeps = SWEEPS - 1
    copies = [sends(sweep) for sweep in range(sweeps)]

    loads[0].wait()
    for s in range(2):
        loads[1 + s].wait()
        rhs = jnp.concatenate([src[s, 0].astype(BF16), src[s, 1].astype(BF16)], axis=1)
        re, im = cprod(pre[s, 0], pre[s, 1], rhs)
        store(st.at[s], re, im)
        if s == 0:
            @pl.when(me > 0)
            def _():
                copies[0][0].start()

    for s in range(2):
        loads[3 + s].wait()
        for p in range(2):
            ct[s, p] = cpl[s, p].T

    for sweep in range(sweeps):
        to_prev, to_next = copies[sweep]
        hr, hi = cprod_adj(ct[1, 0], ct[1, 1], st[1])
        store(hand.at[sweep], hr, hi)

        @pl.when(me < n - 1)
        def _():
            to_next.start()

        lr, li = cprod_adj(ct[0, 0], ct[0, 1], st[0])
        lr = lr.astype(BF16).astype(F32)
        li = li.astype(BF16).astype(F32)
        a1r, a1i = local(1)
        ur, ui = cprod(cpl[0, 0], cpl[0, 1], st[1])
        a0r, a0i = local(0)

        @pl.when(me > 0)
        def _():
            to_next.wait_recv()

        x = arrive[sweep].astype(F32)
        d0 = jnp.concatenate([((a0r + ur) + x[:, :h]).astype(BF16),
                              ((a0i + ui) + x[:, h:]).astype(BF16)], axis=1)

        @pl.when(me > 0)
        def _():
            to_prev.wait_send()

        n0r, n0i = cprod(pre[0, 0], pre[0, 1], d0)
        store(st.at[0], n0r, n0i)
        if sweep + 1 < sweeps:
            @pl.when(me > 0)
            def _():
                copies[sweep + 1][0].start()

        @pl.when(me < n - 1)
        def _():
            to_prev.wait_recv()

        fr, fi = cprod(cpl[1, 0], cpl[1, 1], follow[sweep])
        d1 = jnp.concatenate([((a1r + fr) + lr).astype(BF16),
                              ((a1i + fi) + li).astype(BF16)], axis=1)
        n1r, n1i = cprod(pre[1, 0], pre[1, 1], d1)
        store(st.at[1], n1r, n1i)

        @pl.when(me < n - 1)
        def _():
            to_next.wait_send()

    swap = pltpu.make_async_remote_copy(
        src_ref=st, dst_ref=other, send_sem=swap_sem.at[0], recv_sem=swap_sem.at[1],
        device_id=(mate, me), device_id_type=MESH)
    swap.start()
    out_ref[0] = st[...]
    swap.wait()
    out_ref[1] = other[...]


def solve(precond, coupling, source, sigma, n):
    m, h = source.shape[-2:]
    sweeps = SWEEPS - 1
    half = (m, 2 * h)
    vmem = pl.BlockSpec(memory_space=pltpu.VMEM)
    anyspace = pl.BlockSpec(memory_space=pl.ANY)
    return pl.pallas_call(
        functools.partial(solve_kernel, n),
        out_shape=jax.ShapeDtypeStruct((2, 2) + half, BF16),
        in_specs=[anyspace, anyspace, anyspace, vmem],
        out_specs=vmem,
        scratch_shapes=[
            pltpu.VMEM(precond.shape[1:], BF16),
            pltpu.VMEM(coupling.shape, BF16),
            pltpu.VMEM(source.shape[1:], F32),
            pltpu.VMEM(coupling.shape, BF16),
            pltpu.VMEM((2,) + half, BF16),
            pltpu.VMEM((sweeps,) + half, BF16),
            pltpu.VMEM((sweeps,) + half, BF16),
            pltpu.VMEM((sweeps,) + half, BF16),
            pltpu.VMEM((2,) + half, BF16),
            pltpu.SemaphoreType.DMA((5,)),
            pltpu.SemaphoreType.DMA((2, sweeps)),
            pltpu.SemaphoreType.DMA((2, sweeps)),
            pltpu.SemaphoreType.DMA((2,)),
        ],
        compiler_params=pltpu.CompilerParams(collective_id=0, has_side_effects=True),
    )(precond, coupling, source, sigma)


def nt_dot(a, b):
    return lax.dot_general(a, b, (((1,), (1,)), ((), ())), preferred_element_type=F32)


def self_kernel(both_ref, occ_ref, off_ref, wt_ref, less_ref, great_ref):
    h = both_ref.shape[-1] // 2
    energy_total = occ_ref.shape[0]
    e = lax.axis_index("energy")
    mate = 1 - e
    coef_own = jnp.float32(0.0)
    coef_mate = jnp.float32(0.0)
    for j in range(off_ref.shape[1]):
        t = e + off_ref[e, j]
        inside = jnp.logical_and(t >= 0, t < energy_total)
        w = jnp.where(inside, wt_ref[e, j], jnp.float32(0.0)) / h
        coef_own = coef_own + jnp.where(t == e, w, jnp.float32(0.0))
        coef_mate = coef_mate + jnp.where(t == mate, w, jnp.float32(0.0))
    occ_own = occ_ref[pl.ds(e, 1), :]
    occ_mate = occ_ref[pl.ds(mate, 1), :]
    scales = []
    for own_part, mate_part in ((occ_own, occ_mate), (1.0 - occ_own, 1.0 - occ_mate)):
        so = coef_own * own_part
        sm = coef_mate * mate_part
        scales.append(jnp.concatenate([so, so, sm, sm], axis=1))
    own = both_ref[0, 0]
    mate_states = both_ref[1, 0]
    a = jnp.concatenate([own, mate_states], axis=1)
    swapped = jnp.concatenate(
        [own[:, h:], -own[:, :h], mate_states[:, h:], -mate_states[:, :h]], axis=1)
    af = a.astype(F32)
    for scale, out in zip(scales, (less_ref, great_ref)):
        b = (af * scale).astype(BF16)
        out[0, 0, 0] = nt_dot(a, b).astype(BF16)
        out[0, 0, 1] = nt_dot(swapped, b).astype(BF16)


def self_energy(both, occupation, shift_offsets, shift_weights):
    m, w = both.shape[2:]
    shape = jax.ShapeDtypeStruct((1, 2, 2, m, m), BF16)
    smem = pl.BlockSpec(memory_space=pltpu.SMEM)
    out_spec = pl.BlockSpec((1, 1, 2, m, m), lambda s: (0, s, 0, 0, 0))
    return pl.pallas_call(
        self_kernel,
        out_shape=(shape, shape),
        grid=(2,),
        in_specs=[
            pl.BlockSpec((2, 1, m, w), lambda s: (0, s, 0, 0)),
            pl.BlockSpec(occupation.shape, lambda s: (0, 0)),
            smem,
            smem,
        ],
        out_specs=(out_spec, out_spec),
    )(both, occupation, shift_offsets, shift_weights)


def body(precond, coupling, source, sigma_ret, occupation, shift_offsets, shift_weights):
    n = lax.axis_size("space")
    both = solve(precond, coupling, source, sigma_ret, n)
    return self_energy(both, occupation, shift_offsets, shift_weights)


def solution(mesh):
    placed = (
        P("energy", "space", None, None, None),
        P("space", None, None, None),
        P("energy", "space", None, None, None),
        P("energy", "space", None, None),
        P(),
        P(),
        P(),
    )
    return jax.shard_map(
        body,
        mesh=mesh,
        in_specs=placed,
        out_specs=(P("energy", "space", None, None, None), P("energy", "space", None, None, None)),
        check_vma=False,
    )
```

```python
import functools

import jax
import jax.numpy as jnp
from jax import lax
from jax.experimental import pallas as pl
from jax.experimental.pallas import tpu as pltpu
from jax.sharding import PartitionSpec as P

SWEEPS = 4
MESH = pl.DeviceIdType.MESH
F32 = jnp.float32
BF16 = jnp.bfloat16


def dot(a, b):
    return jnp.dot(a, b, preferred_element_type=F32)


def solve_kernel(n, chunks, pre_hbm, cpl_hbm, src_hbm, sig_ref, out_ref,
                 pre, cpl, src, srcc, ct, st, follow, arrive, hand, other, part,
                 load_sem, send_sem, recv_sem, swap_sem):
    me = lax.axis_index("space")
    en = lax.axis_index("energy")
    prev = lax.rem(me + n - 1, n)
    nxt = lax.rem(me + 1, n)
    mate = 1 - en
    w = st.shape[-1]
    h = w // 2

    loads = [pltpu.make_async_copy(src_hbm.at[0], src, load_sem.at[0])]
    loads += [pltpu.make_async_copy(pre_hbm.at[0, s], pre.at[s], load_sem.at[1 + s]) for s in range(2)]
    loads += [pltpu.make_async_copy(cpl_hbm.at[s], cpl.at[s], load_sem.at[3 + s]) for s in range(2)]
    for c in loads:
        c.start()

    barrier = pltpu.get_barrier_semaphore()
    for peer in ((en, prev), (en, nxt), (mate, me)):
        pl.semaphore_signal(barrier, inc=1, device_id=peer, device_id_type=MESH)
    pl.semaphore_wait(barrier, 3)

    @pl.when(me == n - 1)
    def _():
        follow[...] = jnp.zeros_like(follow)

    @pl.when(me == 0)
    def _():
        arrive[...] = jnp.zeros_like(arrive)

    lanes = lax.broadcasted_iota(jnp.int32, (1, w), 1)
    low = lanes < h
    neg_low = jnp.where(low, -1.0, 1.0).astype(F32)

    def turn(x):
        return pltpu.roll(x, h, 1)

    def column(s):
        g = jnp.concatenate([sig_ref[0, s], jnp.zeros((6, sig_ref.shape[-1]), F32)], axis=0).T
        return g[:, 0:1], g[:, 1:2]

    sig = [column(s) for s in range(2)]

    def cprod(mr, mi, rhs):
        return dot(mr, rhs) + neg_low * turn(dot(mi, rhs))

    def cprod_adj(mr, mi, rhs):
        return dot(mr, rhs) - neg_low * turn(dot(mi, rhs))

    def local(c, s):
        x = st[c, s].astype(F32)
        gr, gi = sig[s]
        return srcc[c, s] + (gr * x + (gi * neg_low) * turn(x))

    sweeps = SWEEPS - 1

    def sends(sweep, c):
        to_prev = pltpu.make_async_remote_copy(
            src_ref=st.at[c, 0], dst_ref=follow.at[sweep, c],
            send_sem=send_sem.at[0, sweep, c], recv_sem=recv_sem.at[0, sweep, c],
            device_id=(en, prev), device_id_type=MESH)
        to_next = pltpu.make_async_remote_copy(
            src_ref=hand.at[sweep, c], dst_ref=arrive.at[sweep, c],
            send_sem=send_sem.at[1, sweep, c], recv_sem=recv_sem.at[1, sweep, c],
            device_id=(en, nxt), device_id_type=MESH)
        return to_prev, to_next

    copies = [[sends(sweep, c) for c in range(chunks)] for sweep in range(sweeps)]

    loads[0].wait()
    for s in range(2):
        re = src[s, 0]
        im = src[s, 1]
        srcc[0, s] = jnp.where(low, re, turn(im))
        srcc[1, s] = jnp.where(low, turn(re), im)

    for s in range(2):
        loads[1 + s].wait()
        for c in range(chunks):
            st[c, s] = cprod(pre[s, 0], pre[s, 1], srcc[c, s].astype(BF16)).astype(BF16)
            if s == 0:
                @pl.when(me > 0)
                def _():
                    copies[0][c][0].start()

    for s in range(2):
        loads[3 + s].wait()
        for p in range(2):
            ct[s, p] = cpl[s, p].T

    def phase1(sweep, c):
        to_prev, to_next = copies[sweep][c]
        hand[sweep, c] = cprod_adj(ct[1, 0], ct[1, 1], st[c, 1]).astype(BF16)

        @pl.when(me < n - 1)
        def _():
            to_next.start()

        part[c, 2] = cprod_adj(ct[0, 0], ct[0, 1], st[c, 0]).astype(BF16).astype(F32)
        part[c, 1] = local(c, 1)
        part[c, 0] = local(c, 0) + cprod(cpl[0, 0], cpl[0, 1], st[c, 1])

    def phase2(sweep, c):
        to_prev, to_next = copies[sweep][c]

        @pl.when(me > 0)
        def _():
            to_next.wait_recv()

        d0 = (part[c, 0] + arrive[sweep, c].astype(F32)).astype(BF16)

        @pl.when(me > 0)
        def _():
            to_prev.wait_send()

        st[c, 0] = cprod(pre[0, 0], pre[0, 1], d0).astype(BF16)
        if sweep + 1 < sweeps:
            @pl.when(me > 0)
            def _():
                copies[sweep + 1][c][0].start()

        @pl.when(me < n - 1)
        def _():
            to_prev.wait_recv()

        upper = cprod(cpl[1, 0], cpl[1, 1], follow[sweep, c])
        d1 = ((part[c, 1] + upper) + part[c, 2]).astype(BF16)
        st[c, 1] = cprod(pre[1, 0], pre[1, 1], d1).astype(BF16)

        @pl.when(me < n - 1)
        def _():
            to_next.wait_send()

    swaps = [pltpu.make_async_remote_copy(
        src_ref=st.at[c], dst_ref=other.at[c], send_sem=swap_sem.at[0, c],
        recv_sem=swap_sem.at[1, c], device_id=(mate, me), device_id_type=MESH)
        for c in range(chunks)]

    for c in range(chunks):
        phase1(0, c)
    for sweep in range(sweeps):
        for c in range(chunks):
            phase2(sweep, c)
            if sweep + 1 < sweeps:
                phase1(sweep + 1, c)
            else:
                swaps[c].start()

    for c in range(chunks):
        for s in range(2):
            out_ref[0, s, :, c * w:(c + 1) * w] = st[c, s]
    for c in range(chunks):
        swaps[c].wait()
        for s in range(2):
            out_ref[1, s, :, c * w:(c + 1) * w] = other[c, s]


def solve(precond, coupling, source, sigma, n):
    m, h = source.shape[-2:]
    chunks = 2
    sweeps = SWEEPS - 1
    blk = (m, 2 * h // chunks)
    vmem = pl.BlockSpec(memory_space=pltpu.VMEM)
    anyspace = pl.BlockSpec(memory_space=pl.ANY)
    return pl.pallas_call(
        functools.partial(solve_kernel, n, chunks),
        out_shape=jax.ShapeDtypeStruct((2, 2, m, 2 * h), BF16),
        in_specs=[anyspace, anyspace, anyspace, vmem],
        out_specs=vmem,
        scratch_shapes=[
            pltpu.VMEM(precond.shape[1:], BF16),
            pltpu.VMEM(coupling.shape, BF16),
            pltpu.VMEM(source.shape[1:], F32),
            pltpu.VMEM((chunks, 2) + blk, F32),
            pltpu.VMEM(coupling.shape, BF16),
            pltpu.VMEM((chunks, 2) + blk, BF16),
            pltpu.VMEM((sweeps, chunks) + blk, BF16),
            pltpu.VMEM((sweeps, chunks) + blk, BF16),
            pltpu.VMEM((sweeps, chunks) + blk, BF16),
            pltpu.VMEM((chunks, 2) + blk, BF16),
            pltpu.VMEM((chunks, 3) + blk, F32),
            pltpu.SemaphoreType.DMA((5,)),
            pltpu.SemaphoreType.DMA((2, sweeps, chunks)),
            pltpu.SemaphoreType.DMA((2, sweeps, chunks)),
            pltpu.SemaphoreType.DMA((2, chunks)),
        ],
        compiler_params=pltpu.CompilerParams(collective_id=0, has_side_effects=True),
    )(precond, coupling, source, sigma)


def nt_dot(a, b):
    return lax.dot_general(a, b, (((1,), (1,)), ((), ())), preferred_element_type=F32)


def self_kernel(both_ref, occ_ref, off_ref, wt_ref, less_ref, great_ref):
    h = both_ref.shape[-1] // 2
    energy_total = occ_ref.shape[0]
    e = lax.axis_index("energy")
    mate = 1 - e
    coef_own = jnp.float32(0.0)
    coef_mate = jnp.float32(0.0)
    for j in range(off_ref.shape[1]):
        t = e + off_ref[e, j]
        inside = jnp.logical_and(t >= 0, t < energy_total)
        w = jnp.where(inside, wt_ref[e, j], jnp.float32(0.0)) / h
        coef_own = coef_own + jnp.where(t == e, w, jnp.float32(0.0))
        coef_mate = coef_mate + jnp.where(t == mate, w, jnp.float32(0.0))
    occ_own = occ_ref[pl.ds(e, 1), :]
    occ_mate = occ_ref[pl.ds(mate, 1), :]
    lanes = lax.broadcasted_iota(jnp.int32, (1, h), 1)
    low = lanes < h // 2
    pos_low = jnp.where(low, 1.0, -1.0).astype(BF16)

    def turn(x):
        return pltpu.roll(x, h // 2, 1)

    def spread(v):
        return jnp.concatenate([jnp.where(low, v, turn(v)), jnp.where(low, turn(v), v)], axis=1)

    scales = []
    for own_part, mate_part in ((occ_own, occ_mate), (1.0 - occ_own, 1.0 - occ_mate)):
        scales.append(jnp.concatenate([spread(coef_own * own_part), spread(coef_mate * mate_part)], axis=1))
    own = both_ref[0, 0]
    mate_states = both_ref[1, 0]
    a = jnp.concatenate([own, mate_states], axis=1)
    blocks = [x[:, i * h:(i + 1) * h] for x in (own, mate_states) for i in range(2)]
    swapped = jnp.concatenate(
        [(turn(b.astype(F32)) * pos_low.astype(F32)).astype(BF16) for b in blocks], axis=1)
    af = a.astype(F32)
    for scale, out in zip(scales, (less_ref, great_ref)):
        b = (af * scale).astype(BF16)
        out[0, 0, 0] = nt_dot(a, b).astype(BF16)
        out[0, 0, 1] = nt_dot(swapped, b).astype(BF16)


def self_energy(both, occupation, shift_offsets, shift_weights):
    m, w = both.shape[2:]
    shape = jax.ShapeDtypeStruct((1, 2, 2, m, m), BF16)
    smem = pl.BlockSpec(memory_space=pltpu.SMEM)
    out_spec = pl.BlockSpec((1, 1, 2, m, m), lambda s: (0, s, 0, 0, 0))
    return pl.pallas_call(
        self_kernel,
        out_shape=(shape, shape),
        grid=(2,),
        in_specs=[
            pl.BlockSpec((2, 1, m, w), lambda s: (0, s, 0, 0)),
            pl.BlockSpec(occupation.shape, lambda s: (0, 0)),
            smem,
            smem,
        ],
        out_specs=(out_spec, out_spec),
    )(both, occupation, shift_offsets, shift_weights)


def body(precond, coupling, source, sigma_ret, occupation, shift_offsets, shift_weights):
    n = lax.axis_size("space")
    both = solve(precond, coupling, source, sigma_ret, n)
    return self_energy(both, occupation, shift_offsets, shift_weights)


def solution(mesh):
    placed = (
        P("energy", "space", None, None, None),
        P("space", None, None, None),
        P("energy", "space", None, None, None),
        P("energy", "space", None, None),
        P(),
        P(),
        P(),
    )
    return jax.shard_map(
        body,
        mesh=mesh,
        in_specs=placed,
        out_specs=(P("energy", "space", None, None, None), P("energy", "space", None, None, None)),
        check_vma=False,
    )
```

```python
import functools

import jax
import jax.numpy as jnp
from jax import lax
from jax.experimental import pallas as pl
from jax.experimental.pallas import tpu as pltpu
from jax.sharding import PartitionSpec as P

SWEEPS = 4
MESH = pl.DeviceIdType.MESH
F32 = jnp.float32
BF16 = jnp.bfloat16


def dot(a, b):
    return jnp.dot(a, b, preferred_element_type=F32)


def exchange_kernel(n, st0_ref, hand_ref, follow_ref, arrive_ref, fbuf, abuf, send_sem, recv_sem):
    me = lax.axis_index("space")
    en = lax.axis_index("energy")
    prev = lax.rem(me + n - 1, n)
    nxt = lax.rem(me + 1, n)
    barrier = pltpu.get_barrier_semaphore()
    for peer in (prev, nxt):
        pl.semaphore_signal(barrier, inc=1, device_id=(en, peer), device_id_type=MESH)
    pl.semaphore_wait(barrier, 2)
    to_prev = pltpu.make_async_remote_copy(
        src_ref=st0_ref, dst_ref=fbuf, send_sem=send_sem.at[0], recv_sem=recv_sem.at[0],
        device_id=(en, prev), device_id_type=MESH)
    to_next = pltpu.make_async_remote_copy(
        src_ref=hand_ref, dst_ref=abuf, send_sem=send_sem.at[1], recv_sem=recv_sem.at[1],
        device_id=(en, nxt), device_id_type=MESH)

    @pl.when(me > 0)
    def _():
        to_prev.start()

    @pl.when(me < n - 1)
    def _():
        to_next.start()

    @pl.when(me < n - 1)
    def _():
        to_prev.wait_recv()
        follow_ref[...] = fbuf[...]

    @pl.when(me == n - 1)
    def _():
        follow_ref[...] = jnp.zeros_like(follow_ref)

    @pl.when(me > 0)
    def _():
        to_next.wait_recv()
        arrive_ref[...] = abuf[...]

    @pl.when(me == 0)
    def _():
        arrive_ref[...] = jnp.zeros_like(arrive_ref)

    @pl.when(me > 0)
    def _():
        to_prev.wait_send()

    @pl.when(me < n - 1)
    def _():
        to_next.wait_send()


def exchange(st0, hand, n, sweep):
    vmem = pl.BlockSpec(memory_space=pltpu.VMEM)
    shape = jax.ShapeDtypeStruct(st0.shape, BF16)
    return pl.pallas_call(
        functools.partial(exchange_kernel, n),
        out_shape=(shape, shape),
        in_specs=[vmem, vmem],
        out_specs=(vmem, vmem),
        scratch_shapes=[
            pltpu.VMEM(st0.shape, BF16),
            pltpu.VMEM(st0.shape, BF16),
            pltpu.SemaphoreType.DMA((2,)),
            pltpu.SemaphoreType.DMA((2,)),
        ],
        compiler_params=pltpu.CompilerParams(collective_id=sweep, has_side_effects=True),
        name=f"exchange_{sweep}",
    )(st0, hand)


def mult(a, b):
    return jnp.einsum("...mn,...nk->...mk", a, b, preferred_element_type=F32)


def mult_adj(a, b):
    return jnp.einsum("...nm,...nk->...mk", a, b, preferred_element_type=F32)


def cprod(m, s):
    re = mult(m[..., 0, :, :], s[..., 0, :, :]) - mult(m[..., 1, :, :], s[..., 1, :, :])
    im = mult(m[..., 0, :, :], s[..., 1, :, :]) + mult(m[..., 1, :, :], s[..., 0, :, :])
    return jnp.stack([re, im], axis=-3)


def cprod_adj(m, s):
    re = mult_adj(m[..., 0, :, :], s[..., 0, :, :]) + mult_adj(m[..., 1, :, :], s[..., 1, :, :])
    im = mult_adj(m[..., 0, :, :], s[..., 1, :, :]) - mult_adj(m[..., 1, :, :], s[..., 0, :, :])
    return jnp.stack([re, im], axis=-3)


def solve(precond, coupling, source, sigma_ret, n):
    pre = precond[0]
    src = source[0]
    states = cprod(pre, src.astype(BF16)).astype(BF16)
    sig_r = sigma_ret[0, :, 0, :, None]
    sig_i = sigma_ret[0, :, 1, :, None]
    for sweep in range(SWEEPS - 1):
        hand = cprod_adj(coupling[1], states[1]).astype(BF16)
        follow, arrive = exchange(states[0], hand, n, sweep)
        beyond = jnp.stack([states[1], follow])
        upper = cprod(coupling, beyond)
        lower = jnp.stack([arrive, cprod_adj(coupling[0], states[0]).astype(BF16)])
        xr = states[:, 0].astype(F32)
        xi = states[:, 1].astype(F32)
        local = jnp.stack([sig_r * xr - sig_i * xi, sig_r * xi + sig_i * xr], axis=1)
        driven = (src + local + upper + lower.astype(F32)).astype(BF16)
        states = cprod(pre, driven).astype(BF16)
    own = jnp.concatenate([states[:, 0], states[:, 1]], axis=-1)
    other = lax.ppermute(own, "energy", [(0, 1), (1, 0)])
    return jnp.stack([own, other])


def nt_dot(a, b):
    return lax.dot_general(a, b, (((1,), (1,)), ((), ())), preferred_element_type=F32)


def self_kernel(both_ref, occ_ref, off_ref, wt_ref, less_ref, great_ref):
    h = both_ref.shape[-1] // 2
    energy_total = occ_ref.shape[0]
    e = lax.axis_index("energy")
    mate = 1 - e
    coef_own = jnp.float32(0.0)
    coef_mate = jnp.float32(0.0)
    for j in range(off_ref.shape[1]):
        t = e + off_ref[e, j]
        inside = jnp.logical_and(t >= 0, t < energy_total)
        w = jnp.where(inside, wt_ref[e, j], jnp.float32(0.0)) / h
        coef_own = coef_own + jnp.where(t == e, w, jnp.float32(0.0))
        coef_mate = coef_mate + jnp.where(t == mate, w, jnp.float32(0.0))
    occ_own = occ_ref[pl.ds(e, 1), :]
    occ_mate = occ_ref[pl.ds(mate, 1), :]
    scales = []
    for own_part, mate_part in ((occ_own, occ_mate), (1.0 - occ_own, 1.0 - occ_mate)):
        so = coef_own * own_part
        sm = coef_mate * mate_part
        scales.append(jnp.concatenate([so, so, sm, sm], axis=1))
    own = both_ref[0, 0]
    mate_states = both_ref[1, 0]
    a = jnp.concatenate([own, mate_states], axis=1)
    swapped = jnp.concatenate(
        [own[:, h:], -own[:, :h], mate_states[:, h:], -mate_states[:, :h]], axis=1)
    af = a.astype(F32)
    for scale, out in zip(scales, (less_ref, great_ref)):
        b = (af * scale).astype(BF16)
        out[0, 0, 0] = nt_dot(a, b).astype(BF16)
        out[0, 0, 1] = nt_dot(swapped, b).astype(BF16)


def self_energy(both, occupation, shift_offsets, shift_weights):
    m, w = both.shape[2:]
    shape = jax.ShapeDtypeStruct((1, 2, 2, m, m), BF16)
    smem = pl.BlockSpec(memory_space=pltpu.SMEM)
    out_spec = pl.BlockSpec((1, 1, 2, m, m), lambda s: (0, s, 0, 0, 0))
    return pl.pallas_call(
        self_kernel,
        out_shape=(shape, shape),
        grid=(2,),
        in_specs=[
            pl.BlockSpec((2, 1, m, w), lambda s: (0, s, 0, 0)),
            pl.BlockSpec(occupation.shape, lambda s: (0, 0)),
            smem,
            smem,
        ],
        out_specs=(out_spec, out_spec),
    )(both, occupation, shift_offsets, shift_weights)


def body(precond, coupling, source, sigma_ret, occupation, shift_offsets, shift_weights):
    n = lax.axis_size("space")
    both = solve(precond, coupling, source, sigma_ret, n)
    return self_energy(both, occupation, shift_offsets, shift_weights)


def solution(mesh):
    placed = (
        P("energy", "space", None, None, None),
        P("space", None, None, None),
        P("energy", "space", None, None, None),
        P("energy", "space", None, None),
        P(),
        P(),
        P(),
    )
    return jax.shard_map(
        body,
        mesh=mesh,
        in_specs=placed,
        out_specs=(P("energy", "space", None, None, None), P("energy", "space", None, None, None)),
        check_vma=False,
    )
```

```python
import functools

import jax
import jax.numpy as jnp
from jax import lax
from jax.experimental import pallas as pl
from jax.experimental.pallas import tpu as pltpu
from jax.sharding import PartitionSpec as P

SWEEPS = 4
MESH = pl.DeviceIdType.MESH
F32 = jnp.float32
BF16 = jnp.bfloat16


def dot(a, b):
    return jnp.dot(a, b, preferred_element_type=F32)


def nt_dot(a, b):
    return lax.dot_general(a, b, (((1,), (1,)), ((), ())), preferred_element_type=F32)


def solve_kernel(n, chunks, pre_hbm, cpl_hbm, src_hbm, sig_ref, out_ref,
                 pre, cpl, src, srcc, st, follow, arrive, hand, other, part,
                 load_sem, send_sem, recv_sem, swap_sem):
    me = lax.axis_index("space")
    en = lax.axis_index("energy")
    prev = lax.rem(me + n - 1, n)
    nxt = lax.rem(me + 1, n)
    mate = 1 - en
    w = st.shape[-2]
    h = w // 2

    loads = [pltpu.make_async_copy(src_hbm.at[0], src, load_sem.at[0])]
    loads += [pltpu.make_async_copy(pre_hbm.at[0, s], pre.at[s], load_sem.at[1 + s]) for s in range(2)]
    loads += [pltpu.make_async_copy(cpl_hbm.at[s], cpl.at[s], load_sem.at[3 + s]) for s in range(2)]
    for c in loads:
        c.start()

    barrier = pltpu.get_barrier_semaphore()
    for peer in ((en, prev), (en, nxt), (mate, me)):
        pl.semaphore_signal(barrier, inc=1, device_id=peer, device_id_type=MESH)
    pl.semaphore_wait(barrier, 3)

    @pl.when(me == n - 1)
    def _():
        follow[...] = jnp.zeros_like(follow)

    @pl.when(me == 0)
    def _():
        arrive[...] = jnp.zeros_like(arrive)

    def cprod(mr, mi, rhs):
        x = nt_dot(rhs, mr)
        y = nt_dot(rhs, mi)
        return jnp.concatenate([x[:h] - y[h:], x[h:] + y[:h]], axis=0)

    def cprod_adj(mr, mi, rhs):
        x = dot(rhs, mr)
        y = dot(rhs, mi)
        return jnp.concatenate([x[:h] + y[h:], x[h:] - y[:h]], axis=0)

    def local(c, s):
        x = st[c, s].astype(F32)
        xr, xi = x[:h], x[h:]
        gr = sig_ref[0, s, pl.ds(0, 1), :]
        gi = sig_ref[0, s, pl.ds(1, 1), :]
        return srcc[c, s] + jnp.concatenate([gr * xr - gi * xi, gr * xi + gi * xr], axis=0)

    sweeps = SWEEPS - 1

    def sends(sweep, c):
        to_prev = pltpu.make_async_remote_copy(
            src_ref=st.at[c, 0], dst_ref=follow.at[sweep, c],
            send_sem=send_sem.at[0, sweep, c], recv_sem=recv_sem.at[0, sweep, c],
            device_id=(en, prev), device_id_type=MESH)
        to_next = pltpu.make_async_remote_copy(
            src_ref=hand.at[sweep, c], dst_ref=arrive.at[sweep, c],
            send_sem=send_sem.at[1, sweep, c], recv_sem=recv_sem.at[1, sweep, c],
            device_id=(en, nxt), device_id_type=MESH)
        return to_prev, to_next

    copies = [[sends(sweep, c) for c in range(chunks)] for sweep in range(sweeps)]

    loads[0].wait()
    for s in range(2):
        re = src[s, 0].T
        im = src[s, 1].T
        for c in range(chunks):
            srcc[c, s] = jnp.concatenate([re[c * h:(c + 1) * h], im[c * h:(c + 1) * h]], axis=0)

    for s in range(2):
        loads[1 + s].wait()
        for c in range(chunks):
            st[c, s] = cprod(pre[s, 0], pre[s, 1], srcc[c, s].astype(BF16)).astype(BF16)
            if s == 0:
                @pl.when(me > 0)
                def _():
                    copies[0][c][0].start()

    for s in range(2):
        loads[3 + s].wait()

    def phase1(sweep, c):
        to_prev, to_next = copies[sweep][c]
        hand[sweep, c] = cprod_adj(cpl[1, 0], cpl[1, 1], st[c, 1]).astype(BF16)

        @pl.when(me < n - 1)
        def _():
            to_next.start()

        part[c, 2] = cprod_adj(cpl[0, 0], cpl[0, 1], st[c, 0]).astype(BF16).astype(F32)
        part[c, 1] = local(c, 1)
        part[c, 0] = local(c, 0) + cprod(cpl[0, 0], cpl[0, 1], st[c, 1])

    def phase2(sweep, c):
        to_prev, to_next = copies[sweep][c]

        @pl.when(me > 0)
        def _():
            to_next.wait_recv()

        d0 = (part[c, 0] + arrive[sweep, c].astype(F32)).astype(BF16)

        @pl.when(me > 0)
        def _():
            to_prev.wait_send()

        st[c, 0] = cprod(pre[0, 0], pre[0, 1], d0).astype(BF16)
        if sweep + 1 < sweeps:
            @pl.when(me > 0)
            def _():
                copies[sweep + 1][c][0].start()

        @pl.when(me < n - 1)
        def _():
            to_prev.wait_recv()

        upper = cprod(cpl[1, 0], cpl[1, 1], follow[sweep, c])
        d1 = ((part[c, 1] + upper) + part[c, 2]).astype(BF16)
        st[c, 1] = cprod(pre[1, 0], pre[1, 1], d1).astype(BF16)

        @pl.when(me < n - 1)
        def _():
            to_next.wait_send()

    swaps = [pltpu.make_async_remote_copy(
        src_ref=st.at[c], dst_ref=other.at[c], send_sem=swap_sem.at[0, c],
        recv_sem=swap_sem.at[1, c], device_id=(mate, me), device_id_type=MESH)
        for c in range(chunks)]

    for c in range(chunks):
        phase1(0, c)
    for sweep in range(sweeps):
        for c in range(chunks):
            phase2(sweep, c)
            if sweep + 1 < sweeps:
                phase1(sweep + 1, c)
            else:
                swaps[c].start()

    for c in range(chunks):
        for s in range(2):
            out_ref[0, s, :, c * w:(c + 1) * w] = st[c, s].T
    for c in range(chunks):
        swaps[c].wait()
        for s in range(2):
            out_ref[1, s, :, c * w:(c + 1) * w] = other[c, s].T


def solve(precond, coupling, source, sigma, n):
    m, h = source.shape[-2:]
    chunks = 2
    sweeps = SWEEPS - 1
    blk = (2 * h // chunks, m)
    vmem = pl.BlockSpec(memory_space=pltpu.VMEM)
    anyspace = pl.BlockSpec(memory_space=pl.ANY)
    return pl.pallas_call(
        functools.partial(solve_kernel, n, chunks),
        out_shape=jax.ShapeDtypeStruct((2, 2, m, 2 * h), BF16),
        in_specs=[anyspace, anyspace, anyspace, vmem],
        out_specs=vmem,
        scratch_shapes=[
            pltpu.VMEM(precond.shape[1:], BF16),
            pltpu.VMEM(coupling.shape, BF16),
            pltpu.VMEM(source.shape[1:], F32),
            pltpu.VMEM((chunks, 2) + blk, F32),
            pltpu.VMEM((chunks, 2) + blk, BF16),
            pltpu.VMEM((sweeps, chunks) + blk, BF16),
            pltpu.VMEM((sweeps, chunks) + blk, BF16),
            pltpu.VMEM((sweeps, chunks) + blk, BF16),
            pltpu.VMEM((chunks, 2) + blk, BF16),
            pltpu.VMEM((chunks, 3) + blk, F32),
            pltpu.SemaphoreType.DMA((5,)),
            pltpu.SemaphoreType.DMA((2, sweeps, chunks)),
            pltpu.SemaphoreType.DMA((2, sweeps, chunks)),
            pltpu.SemaphoreType.DMA((2, chunks)),
        ],
        compiler_params=pltpu.CompilerParams(collective_id=0, has_side_effects=True),
    )(precond, coupling, source, sigma)


def self_kernel(both_ref, occ_ref, off_ref, wt_ref, less_ref, great_ref):
    h = both_ref.shape[-1] // 2
    energy_total = occ_ref.shape[0]
    e = lax.axis_index("energy")
    mate = 1 - e
    coef_own = jnp.float32(0.0)
    coef_mate = jnp.float32(0.0)
    for j in range(off_ref.shape[1]):
        t = e + off_ref[e, j]
        inside = jnp.logical_and(t >= 0, t < energy_total)
        w = jnp.where(inside, wt_ref[e, j], jnp.float32(0.0)) / h
        coef_own = coef_own + jnp.where(t == e, w, jnp.float32(0.0))
        coef_mate = coef_mate + jnp.where(t == mate, w, jnp.float32(0.0))
    occ_own = occ_ref[pl.ds(e, 1), :]
    occ_mate = occ_ref[pl.ds(mate, 1), :]
    lanes = lax.broadcasted_iota(jnp.int32, (1, h), 1)
    low = lanes < h // 2
    pos_low = jnp.where(low, 1.0, -1.0).astype(BF16)

    def turn(x):
        return pltpu.roll(x, h // 2, 1)

    def spread(v):
        return jnp.concatenate([jnp.where(low, v, turn(v)), jnp.where(low, turn(v), v)], axis=1)

    scales = []
    for own_part, mate_part in ((occ_own, occ_mate), (1.0 - occ_own, 1.0 - occ_mate)):
        scales.append(jnp.concatenate([spread(coef_own * own_part), spread(coef_mate * mate_part)], axis=1))
    own = both_ref[0, 0]
    mate_states = both_ref[1, 0]
    a = jnp.concatenate([own, mate_states], axis=1)
    blocks = [x[:, i * h:(i + 1) * h] for x in (own, mate_states) for i in range(2)]
    swapped = jnp.concatenate(
        [(turn(b.astype(F32)) * pos_low.astype(F32)).astype(BF16) for b in blocks], axis=1)
    af = a.astype(F32)
    for scale, out in zip(scales, (less_ref, great_ref)):
        b = (af * scale).astype(BF16)
        out[0, 0, 0] = nt_dot(a, b).astype(BF16)
        out[0, 0, 1] = nt_dot(swapped, b).astype(BF16)


def self_energy(both, occupation, shift_offsets, shift_weights):
    m, w = both.shape[2:]
    shape = jax.ShapeDtypeStruct((1, 2, 2, m, m), BF16)
    smem = pl.BlockSpec(memory_space=pltpu.SMEM)
    out_spec = pl.BlockSpec((1, 1, 2, m, m), lambda s: (0, s, 0, 0, 0))
    return pl.pallas_call(
        self_kernel,
        out_shape=(shape, shape),
        grid=(2,),
        in_specs=[
            pl.BlockSpec((2, 1, m, w), lambda s: (0, s, 0, 0)),
            pl.BlockSpec(occupation.shape, lambda s: (0, 0)),
            smem,
            smem,
        ],
        out_specs=(out_spec, out_spec),
    )(both, occupation, shift_offsets, shift_weights)


def body(precond, coupling, source, sigma_ret, occupation, shift_offsets, shift_weights):
    n = lax.axis_size("space")
    both = solve(precond, coupling, source, sigma_ret, n)
    return self_energy(both, occupation, shift_offsets, shift_weights)


def solution(mesh):
    placed = (
        P("energy", "space", None, None, None),
        P("space", None, None, None),
        P("energy", "space", None, None, None),
        P("energy", "space", None, None),
        P(),
        P(),
        P(),
    )
    return jax.shard_map(
        body,
        mesh=mesh,
        in_specs=placed,
        out_specs=(P("energy", "space", None, None, None), P("energy", "space", None, None, None)),
        check_vma=False,
    )
```

```python
import functools

import jax
import jax.numpy as jnp
from jax import lax
from jax.experimental import pallas as pl
from jax.experimental.pallas import tpu as pltpu
from jax.sharding import PartitionSpec as P

SWEEPS = 4
MESH = pl.DeviceIdType.MESH
F32 = jnp.float32
BF16 = jnp.bfloat16


def dot(a, b):
    return jnp.dot(a, b, preferred_element_type=F32)


def nt_dot(a, b):
    return lax.dot_general(a, b, (((1,), (1,)), ((), ())), preferred_element_type=F32)


def solve_kernel(n, chunks, pre_hbm, cpl_hbm, src_hbm, sig_ref, occ_ref, off_ref, wt_ref,
                 out_ref, scale_ref,
                 pre, cpl, src, srcc, st, follow, arrive, hand, other, part,
                 load_sem, send_sem, recv_sem, swap_sem):
    me = lax.axis_index("space")
    en = lax.axis_index("energy")
    prev = lax.rem(me + n - 1, n)
    nxt = lax.rem(me + 1, n)
    mate = 1 - en
    w = st.shape[-2]
    h = w // 2

    loads = [pltpu.make_async_copy(src_hbm.at[0], src, load_sem.at[0])]
    loads += [pltpu.make_async_copy(pre_hbm.at[0, s], pre.at[s], load_sem.at[1 + s]) for s in range(2)]
    loads += [pltpu.make_async_copy(cpl_hbm.at[s], cpl.at[s], load_sem.at[3 + s]) for s in range(2)]
    for c in loads:
        c.start()

    barrier = pltpu.get_barrier_semaphore()
    for peer in ((en, prev), (en, nxt), (mate, me)):
        pl.semaphore_signal(barrier, inc=1, device_id=peer, device_id_type=MESH)
    pl.semaphore_wait(barrier, 3)

    shift_scales(occ_ref, off_ref, wt_ref, scale_ref)

    @pl.when(me == n - 1)
    def _():
        follow[...] = jnp.zeros_like(follow)

    @pl.when(me == 0)
    def _():
        arrive[...] = jnp.zeros_like(arrive)

    def cprod(mr, mi, rhs):
        x = nt_dot(rhs, mr)
        y = nt_dot(rhs, mi)
        return jnp.concatenate([x[:h] - y[h:], x[h:] + y[:h]], axis=0)

    def cprod_adj(mr, mi, rhs):
        x = dot(rhs, mr)
        y = dot(rhs, mi)
        return jnp.concatenate([x[:h] + y[h:], x[h:] - y[:h]], axis=0)

    def local(c, s):
        x = st[c, s].astype(F32)
        xr, xi = x[:h], x[h:]
        gr = sig_ref[0, s, pl.ds(0, 1), :]
        gi = sig_ref[0, s, pl.ds(1, 1), :]
        return srcc[c, s] + jnp.concatenate([gr * xr - gi * xi, gr * xi + gi * xr], axis=0)

    sweeps = SWEEPS - 1

    def sends(sweep, c):
        to_prev = pltpu.make_async_remote_copy(
            src_ref=st.at[c, 0], dst_ref=follow.at[sweep, c],
            send_sem=send_sem.at[0, sweep, c], recv_sem=recv_sem.at[0, sweep, c],
            device_id=(en, prev), device_id_type=MESH)
        to_next = pltpu.make_async_remote_copy(
            src_ref=hand.at[sweep, c], dst_ref=arrive.at[sweep, c],
            send_sem=send_sem.at[1, sweep, c], recv_sem=recv_sem.at[1, sweep, c],
            device_id=(en, nxt), device_id_type=MESH)
        return to_prev, to_next

    copies = [[sends(sweep, c) for c in range(chunks)] for sweep in range(sweeps)]

    loads[0].wait()
    for s in range(2):
        re = src[s, 0].T
        im = src[s, 1].T
        for c in range(chunks):
            srcc[c, s] = jnp.concatenate([re[c * h:(c + 1) * h], im[c * h:(c + 1) * h]], axis=0)

    for s in range(2):
        loads[1 + s].wait()
        for c in range(chunks):
            st[c, s] = cprod(pre[s, 0], pre[s, 1], srcc[c, s].astype(BF16)).astype(BF16)
            if s == 0:
                @pl.when(me > 0)
                def _():
                    copies[0][c][0].start()

    for s in range(2):
        loads[3 + s].wait()

    def phase1(sweep, c):
        to_prev, to_next = copies[sweep][c]
        hand[sweep, c] = cprod_adj(cpl[1, 0], cpl[1, 1], st[c, 1]).astype(BF16)

        @pl.when(me < n - 1)
        def _():
            to_next.start()

        part[c, 2] = cprod_adj(cpl[0, 0], cpl[0, 1], st[c, 0]).astype(BF16).astype(F32)
        part[c, 1] = local(c, 1)
        part[c, 0] = local(c, 0) + cprod(cpl[0, 0], cpl[0, 1], st[c, 1])

    def phase2(sweep, c):
        to_prev, to_next = copies[sweep][c]

        @pl.when(me > 0)
        def _():
            to_next.wait_recv()

        d0 = (part[c, 0] + arrive[sweep, c].astype(F32)).astype(BF16)

        @pl.when(me > 0)
        def _():
            to_prev.wait_send()

        st[c, 0] = cprod(pre[0, 0], pre[0, 1], d0).astype(BF16)
        if sweep + 1 < sweeps:
            @pl.when(me > 0)
            def _():
                copies[sweep + 1][c][0].start()

        @pl.when(me < n - 1)
        def _():
            to_prev.wait_recv()

        upper = cprod(cpl[1, 0], cpl[1, 1], follow[sweep, c])
        d1 = ((part[c, 1] + upper) + part[c, 2]).astype(BF16)
        st[c, 1] = cprod(pre[1, 0], pre[1, 1], d1).astype(BF16)

        @pl.when(me < n - 1)
        def _():
            to_next.wait_send()

    swaps = [pltpu.make_async_remote_copy(
        src_ref=st.at[c], dst_ref=other.at[c], send_sem=swap_sem.at[0, c],
        recv_sem=swap_sem.at[1, c], device_id=(mate, me), device_id_type=MESH)
        for c in range(chunks)]

    for c in range(chunks):
        phase1(0, c)
    for sweep in range(sweeps):
        for c in range(chunks):
            phase2(sweep, c)
            if sweep + 1 < sweeps:
                phase1(sweep + 1, c)
            else:
                swaps[c].start()

    for c in range(chunks):
        for s in range(2):
            out_ref[0, s, :, c * w:(c + 1) * w] = st[c, s].T
    for c in range(chunks):
        swaps[c].wait()
        for s in range(2):
            out_ref[1, s, :, c * w:(c + 1) * w] = other[c, s].T


def solve(precond, coupling, source, sigma, occupation, shift_offsets, shift_weights, n):
    m, h = source.shape[-2:]
    chunks = 2
    sweeps = SWEEPS - 1
    blk = (2 * h // chunks, m)
    vmem = pl.BlockSpec(memory_space=pltpu.VMEM)
    anyspace = pl.BlockSpec(memory_space=pl.ANY)
    smem = pl.BlockSpec(memory_space=pltpu.SMEM)
    return pl.pallas_call(
        functools.partial(solve_kernel, n, chunks),
        out_shape=(jax.ShapeDtypeStruct((2, 2, m, 2 * h), BF16),
                   jax.ShapeDtypeStruct((2, 1, 4 * h), F32)),
        in_specs=[anyspace, anyspace, anyspace, vmem, vmem, smem, smem],
        out_specs=(vmem, vmem),
        scratch_shapes=[
            pltpu.VMEM(precond.shape[1:], BF16),
            pltpu.VMEM(coupling.shape, BF16),
            pltpu.VMEM(source.shape[1:], F32),
            pltpu.VMEM((chunks, 2) + blk, F32),
            pltpu.VMEM((chunks, 2) + blk, BF16),
            pltpu.VMEM((sweeps, chunks) + blk, BF16),
            pltpu.VMEM((sweeps, chunks) + blk, BF16),
            pltpu.VMEM((sweeps, chunks) + blk, BF16),
            pltpu.VMEM((chunks, 2) + blk, BF16),
            pltpu.VMEM((chunks, 3) + blk, F32),
            pltpu.SemaphoreType.DMA((5,)),
            pltpu.SemaphoreType.DMA((2, sweeps, chunks)),
            pltpu.SemaphoreType.DMA((2, sweeps, chunks)),
            pltpu.SemaphoreType.DMA((2, chunks)),
        ],
        compiler_params=pltpu.CompilerParams(collective_id=0, has_side_effects=True),
    )(precond, coupling, source, sigma, occupation, shift_offsets, shift_weights)


def shift_scales(occ_ref, off_ref, wt_ref, scale_ref):
    h = occ_ref.shape[-1]
    energy_total = occ_ref.shape[0]
    e = lax.axis_index("energy")
    mate = 1 - e
    coef_own = jnp.float32(0.0)
    coef_mate = jnp.float32(0.0)
    for j in range(off_ref.shape[1]):
        t = e + off_ref[e, j]
        inside = jnp.logical_and(t >= 0, t < energy_total)
        w = jnp.where(inside, wt_ref[e, j], jnp.float32(0.0)) / h
        coef_own = coef_own + jnp.where(t == e, w, jnp.float32(0.0))
        coef_mate = coef_mate + jnp.where(t == mate, w, jnp.float32(0.0))
    occ_own = occ_ref[pl.ds(e, 1), :]
    occ_mate = occ_ref[pl.ds(mate, 1), :]
    lanes = lax.broadcasted_iota(jnp.int32, (1, h), 1)
    low = lanes < h // 2

    def turn(x):
        return pltpu.roll(x, h // 2, 1)

    def spread(v):
        return jnp.concatenate([jnp.where(low, v, turn(v)), jnp.where(low, turn(v), v)], axis=1)

    pairs = ((occ_own, occ_mate), (1.0 - occ_own, 1.0 - occ_mate))
    for q, (own_part, mate_part) in enumerate(pairs):
        scale_ref[q] = jnp.concatenate(
            [spread(coef_own * own_part), spread(coef_mate * mate_part)], axis=1)


def self_energy(both, scales):
    a = jnp.concatenate([both[0], both[1]], axis=-1)
    s, m, k = a.shape
    width = both.shape[-1] // 2
    halves = a.reshape(s, m, k // width, 2, width // 2)
    swapped = jnp.stack([halves[:, :, :, 1], -halves[:, :, :, 0]], axis=3).reshape(s, m, k)
    lhs = jnp.stack([a, swapped], axis=1)
    af = a.astype(F32)
    outs = []
    for i in range(2):
        b = (af * scales[i]).astype(BF16)
        out = jnp.einsum("scmk,snk->scmn", lhs, b, preferred_element_type=F32)
        outs.append(out.astype(BF16)[None])
    return tuple(outs)


def body(precond, coupling, source, sigma_ret, occupation, shift_offsets, shift_weights):
    n = lax.axis_size("space")
    both, scales = solve(precond, coupling, source, sigma_ret, occupation, shift_offsets,
                         shift_weights, n)
    return self_energy(both, scales)


def solution(mesh):
    placed = (
        P("energy", "space", None, None, None),
        P("space", None, None, None),
        P("energy", "space", None, None, None),
        P("energy", "space", None, None),
        P(),
        P(),
        P(),
    )
    return jax.shard_map(
        body,
        mesh=mesh,
        in_specs=placed,
        out_specs=(P("energy", "space", None, None, None), P("energy", "space", None, None, None)),
        check_vma=False,
    )
```

```python
import functools

import jax
import jax.numpy as jnp
from jax import lax
from jax.experimental import pallas as pl
from jax.experimental.pallas import tpu as pltpu
from jax.sharding import PartitionSpec as P

SWEEPS = 4
MESH = pl.DeviceIdType.MESH
F32 = jnp.float32
BF16 = jnp.bfloat16


def dot(a, b):
    return jnp.dot(a, b, preferred_element_type=F32)


def nt_dot(a, b):
    return lax.dot_general(a, b, (((1,), (1,)), ((), ())), preferred_element_type=F32)


def solve_kernel(n, chunks, pre_hbm, cpl_hbm, src_hbm, sig_ref, out_ref,
                 pre, cpl, src, srcc, st, follow, arrive, hand, other, part,
                 load_sem, send_sem, recv_sem, swap_sem):
    me = lax.axis_index("space")
    en = lax.axis_index("energy")
    prev = lax.rem(me + n - 1, n)
    nxt = lax.rem(me + 1, n)
    mate = 1 - en
    w = st.shape[-2]
    h = w // 2

    loads = [pltpu.make_async_copy(src_hbm.at[0], src, load_sem.at[0])]
    loads += [pltpu.make_async_copy(pre_hbm.at[0, s], pre.at[s], load_sem.at[1 + s]) for s in range(2)]
    loads += [pltpu.make_async_copy(cpl_hbm.at[s], cpl.at[s], load_sem.at[3 + s]) for s in range(2)]
    for c in loads:
        c.start()

    barrier = pltpu.get_barrier_semaphore()
    for peer in ((en, prev), (en, nxt), (mate, me)):
        pl.semaphore_signal(barrier, inc=1, device_id=peer, device_id_type=MESH)
    pl.semaphore_wait(barrier, 3)

    @pl.when(me == n - 1)
    def _():
        follow[...] = jnp.zeros_like(follow)

    @pl.when(me == 0)
    def _():
        arrive[...] = jnp.zeros_like(arrive)

    def cprod(mr, mi, rhs):
        x = nt_dot(rhs, mr)
        y = nt_dot(rhs, mi)
        return jnp.concatenate([x[:h] - y[h:], x[h:] + y[:h]], axis=0)

    def cprod_adj(mr, mi, rhs):
        x = dot(rhs, mr)
        y = dot(rhs, mi)
        return jnp.concatenate([x[:h] + y[h:], x[h:] - y[:h]], axis=0)

    def local(c, s):
        x = st[c, s].astype(F32)
        xr, xi = x[:h], x[h:]
        gr = sig_ref[0, s, pl.ds(0, 1), :]
        gi = sig_ref[0, s, pl.ds(1, 1), :]
        return srcc[c, s] + jnp.concatenate([gr * xr - gi * xi, gr * xi + gi * xr], axis=0)

    sweeps = SWEEPS - 1

    def sends(sweep, c):
        to_prev = pltpu.make_async_remote_copy(
            src_ref=st.at[c, 0], dst_ref=follow.at[sweep, c],
            send_sem=send_sem.at[0, sweep, c], recv_sem=recv_sem.at[0, sweep, c],
            device_id=(en, prev), device_id_type=MESH)
        to_next = pltpu.make_async_remote_copy(
            src_ref=hand.at[sweep, c], dst_ref=arrive.at[sweep, c],
            send_sem=send_sem.at[1, sweep, c], recv_sem=recv_sem.at[1, sweep, c],
            device_id=(en, nxt), device_id_type=MESH)
        return to_prev, to_next

    copies = [[sends(sweep, c) for c in range(chunks)] for sweep in range(sweeps)]

    loads[0].wait()
    for s in range(2):
        re = src[s, 0].T
        im = src[s, 1].T
        for c in range(chunks):
            srcc[c, s] = jnp.concatenate([re[c * h:(c + 1) * h], im[c * h:(c + 1) * h]], axis=0)

    for s in range(2):
        loads[1 + s].wait()
        for c in range(chunks):
            st[c, s] = cprod(pre[s, 0], pre[s, 1], srcc[c, s].astype(BF16)).astype(BF16)
            if s == 0:
                @pl.when(me > 0)
                def _():
                    copies[0][c][0].start()

    for s in range(2):
        loads[3 + s].wait()

    def phase1(sweep, c):
        to_prev, to_next = copies[sweep][c]
        hand[sweep, c] = cprod_adj(cpl[1, 0], cpl[1, 1], st[c, 1]).astype(BF16)

        @pl.when(me < n - 1)
        def _():
            to_next.start()

        part[c, 2] = cprod_adj(cpl[0, 0], cpl[0, 1], st[c, 0]).astype(BF16).astype(F32)
        part[c, 1] = local(c, 1)
        part[c, 0] = local(c, 0) + cprod(cpl[0, 0], cpl[0, 1], st[c, 1])

    def phase2(sweep, c):
        to_prev, to_next = copies[sweep][c]

        @pl.when(me > 0)
        def _():
            to_next.wait_recv()

        d0 = (part[c, 0] + arrive[sweep, c].astype(F32)).astype(BF16)

        @pl.when(me > 0)
        def _():
            to_prev.wait_send()

        st[c, 0] = cprod(pre[0, 0], pre[0, 1], d0).astype(BF16)
        if sweep + 1 < sweeps:
            @pl.when(me > 0)
            def _():
                copies[sweep + 1][c][0].start()

        @pl.when(me < n - 1)
        def _():
            to_prev.wait_recv()

        upper = cprod(cpl[1, 0], cpl[1, 1], follow[sweep, c])
        d1 = ((part[c, 1] + upper) + part[c, 2]).astype(BF16)
        st[c, 1] = cprod(pre[1, 0], pre[1, 1], d1).astype(BF16)

        @pl.when(me < n - 1)
        def _():
            to_next.wait_send()

    swaps = [pltpu.make_async_remote_copy(
        src_ref=st.at[c], dst_ref=other.at[c], send_sem=swap_sem.at[0, c],
        recv_sem=swap_sem.at[1, c], device_id=(mate, me), device_id_type=MESH)
        for c in range(chunks)]

    for c in range(chunks):
        phase1(0, c)
    for sweep in range(sweeps):
        for c in range(chunks):
            phase2(sweep, c)
            if sweep + 1 < sweeps:
                phase1(sweep + 1, c)
            else:
                swaps[c].start()

    q = out_ref.shape[-1] // 4
    per = h // q

    def put(i, ref, c):
        for s in range(2):
            x = ref[c, s]
            for b in range(per):
                rows = jnp.concatenate([x[b * q:(b + 1) * q], x[h + b * q:h + (b + 1) * q]], axis=0)
                lo = (c * per + b) * 2 * q
                out_ref[i, s, :, lo:lo + 2 * q] = rows.T

    for c in range(chunks):
        put(0, st, c)
    for c in range(chunks):
        swaps[c].wait()
        put(1, other, c)


def solve(precond, coupling, source, sigma, n):
    m, h = source.shape[-2:]
    chunks = 1
    sweeps = SWEEPS - 1
    blk = (2 * h // chunks, m)
    vmem = pl.BlockSpec(memory_space=pltpu.VMEM)
    anyspace = pl.BlockSpec(memory_space=pl.ANY)
    return pl.pallas_call(
        functools.partial(solve_kernel, n, chunks),
        out_shape=jax.ShapeDtypeStruct((2, 2, m, 2 * h), BF16),
        in_specs=[anyspace, anyspace, anyspace, vmem],
        out_specs=vmem,
        scratch_shapes=[
            pltpu.VMEM(precond.shape[1:], BF16),
            pltpu.VMEM(coupling.shape, BF16),
            pltpu.VMEM(source.shape[1:], F32),
            pltpu.VMEM((chunks, 2) + blk, F32),
            pltpu.VMEM((chunks, 2) + blk, BF16),
            pltpu.VMEM((sweeps, chunks) + blk, BF16),
            pltpu.VMEM((sweeps, chunks) + blk, BF16),
            pltpu.VMEM((sweeps, chunks) + blk, BF16),
            pltpu.VMEM((chunks, 2) + blk, BF16),
            pltpu.VMEM((chunks, 3) + blk, F32),
            pltpu.SemaphoreType.DMA((5,)),
            pltpu.SemaphoreType.DMA((2, sweeps, chunks)),
            pltpu.SemaphoreType.DMA((2, sweeps, chunks)),
            pltpu.SemaphoreType.DMA((2, chunks)),
        ],
        compiler_params=pltpu.CompilerParams(collective_id=0, has_side_effects=True),
    )(precond, coupling, source, sigma)


def self_kernel(both_ref, occ_ref, off_ref, wt_ref, less_ref, great_ref):
    h = both_ref.shape[-1] // 2
    energy_total = occ_ref.shape[0]
    e = lax.axis_index("energy")
    mate = 1 - e
    coef_own = jnp.float32(0.0)
    coef_mate = jnp.float32(0.0)
    for j in range(off_ref.shape[1]):
        t = e + off_ref[e, j]
        inside = jnp.logical_and(t >= 0, t < energy_total)
        w = jnp.where(inside, wt_ref[e, j], jnp.float32(0.0)) / h
        coef_own = coef_own + jnp.where(t == e, w, jnp.float32(0.0))
        coef_mate = coef_mate + jnp.where(t == mate, w, jnp.float32(0.0))
    occ_own = occ_ref[pl.ds(e, 1), :]
    occ_mate = occ_ref[pl.ds(mate, 1), :]
    lanes = lax.broadcasted_iota(jnp.int32, (1, h), 1)
    low = lanes < h // 2
    pos_low = jnp.where(low, 1.0, -1.0).astype(BF16)

    def turn(x):
        return pltpu.roll(x, h // 2, 1)

    def spread(v):
        return jnp.concatenate([jnp.where(low, v, turn(v)), jnp.where(low, turn(v), v)], axis=1)

    scales = []
    for own_part, mate_part in ((occ_own, occ_mate), (1.0 - occ_own, 1.0 - occ_mate)):
        scales.append(jnp.concatenate([spread(coef_own * own_part), spread(coef_mate * mate_part)], axis=1))
    own = both_ref[0, 0]
    mate_states = both_ref[1, 0]
    a = jnp.concatenate([own, mate_states], axis=1)
    blocks = [x[:, i * h:(i + 1) * h] for x in (own, mate_states) for i in range(2)]
    swapped = jnp.concatenate(
        [(turn(b.astype(F32)) * pos_low.astype(F32)).astype(BF16) for b in blocks], axis=1)
    af = a.astype(F32)
    for scale, out in zip(scales, (less_ref, great_ref)):
        b = (af * scale).astype(BF16)
        out[0, 0, 0] = nt_dot(a, b).astype(BF16)
        out[0, 0, 1] = nt_dot(swapped, b).astype(BF16)


def self_energy(both, occupation, shift_offsets, shift_weights):
    m, w = both.shape[2:]
    shape = jax.ShapeDtypeStruct((1, 2, 2, m, m), BF16)
    smem = pl.BlockSpec(memory_space=pltpu.SMEM)
    out_spec = pl.BlockSpec((1, 1, 2, m, m), lambda s: (0, s, 0, 0, 0))
    return pl.pallas_call(
        self_kernel,
        out_shape=(shape, shape),
        grid=(2,),
        in_specs=[
            pl.BlockSpec((2, 1, m, w), lambda s: (0, s, 0, 0)),
            pl.BlockSpec(occupation.shape, lambda s: (0, 0)),
            smem,
            smem,
        ],
        out_specs=(out_spec, out_spec),
    )(both, occupation, shift_offsets, shift_weights)


def body(precond, coupling, source, sigma_ret, occupation, shift_offsets, shift_weights):
    n = lax.axis_size("space")
    both = solve(precond, coupling, source, sigma_ret, n)
    return self_energy(both, occupation, shift_offsets, shift_weights)


def solution(mesh):
    placed = (
        P("energy", "space", None, None, None),
        P("space", None, None, None),
        P("energy", "space", None, None, None),
        P("energy", "space", None, None),
        P(),
        P(),
        P(),
    )
    return jax.shard_map(
        body,
        mesh=mesh,
        in_specs=placed,
        out_specs=(P("energy", "space", None, None, None), P("energy", "space", None, None, None)),
        check_vma=False,
    )
```

```python
import functools

import jax
import jax.numpy as jnp
from jax import lax
from jax.experimental import pallas as pl
from jax.experimental.pallas import tpu as pltpu
from jax.sharding import PartitionSpec as P

SWEEPS = 4
MESH = pl.DeviceIdType.MESH
F32 = jnp.float32
BF16 = jnp.bfloat16


def dot(a, b):
    return jnp.dot(a, b, preferred_element_type=F32)


def nt_dot(a, b):
    return lax.dot_general(a, b, (((1,), (1,)), ((), ())), preferred_element_type=F32)


def solve_kernel(n, chunks, pre_hbm, cpl_hbm, src_hbm, sig_ref, out_ref,
                 pre, cpl, src, srcc, st, follow, arrive, hand, other, part,
                 load_sem, send_sem, recv_sem, swap_sem):
    me = lax.axis_index("space")
    en = lax.axis_index("energy")
    prev = lax.rem(me + n - 1, n)
    nxt = lax.rem(me + 1, n)
    mate = 1 - en
    w = st.shape[-2]
    h = w // 2

    loads = [pltpu.make_async_copy(src_hbm.at[0], src, load_sem.at[0])]
    loads += [pltpu.make_async_copy(pre_hbm.at[0, s], pre.at[s], load_sem.at[1 + s]) for s in range(2)]
    loads += [pltpu.make_async_copy(cpl_hbm.at[s], cpl.at[s], load_sem.at[3 + s]) for s in range(2)]
    for c in loads:
        c.start()

    barrier = pltpu.get_barrier_semaphore()
    for peer in ((en, prev), (en, nxt), (mate, me)):
        pl.semaphore_signal(barrier, inc=1, device_id=peer, device_id_type=MESH)
    pl.semaphore_wait(barrier, 3)

    @pl.when(me == n - 1)
    def _():
        follow[...] = jnp.zeros_like(follow)

    @pl.when(me == 0)
    def _():
        arrive[...] = jnp.zeros_like(arrive)

    def cprod(mr, mi, rhs):
        x = nt_dot(rhs, mr)
        y = nt_dot(rhs, mi)
        return jnp.concatenate([x[:h] - y[h:], x[h:] + y[:h]], axis=0)

    def cprod_adj(mr, mi, rhs):
        x = dot(rhs, mr)
        y = dot(rhs, mi)
        return jnp.concatenate([x[:h] + y[h:], x[h:] - y[:h]], axis=0)

    def local(c, s):
        x = st[c, s].astype(F32)
        xr, xi = x[:h], x[h:]
        gr = sig_ref[0, s, pl.ds(0, 1), :]
        gi = sig_ref[0, s, pl.ds(1, 1), :]
        return srcc[c, s] + jnp.concatenate([gr * xr - gi * xi, gr * xi + gi * xr], axis=0)

    sweeps = SWEEPS - 1

    def sends(sweep, c):
        to_prev = pltpu.make_async_remote_copy(
            src_ref=st.at[c, 0], dst_ref=follow.at[sweep, c],
            send_sem=send_sem.at[0, sweep, c], recv_sem=recv_sem.at[0, sweep, c],
            device_id=(en, prev), device_id_type=MESH)
        to_next = pltpu.make_async_remote_copy(
            src_ref=hand.at[sweep, c], dst_ref=arrive.at[sweep, c],
            send_sem=send_sem.at[1, sweep, c], recv_sem=recv_sem.at[1, sweep, c],
            device_id=(en, nxt), device_id_type=MESH)
        return to_prev, to_next

    copies = [[sends(sweep, c) for c in range(chunks)] for sweep in range(sweeps)]

    loads[0].wait()
    for s in range(2):
        re = src[s, 0].T
        im = src[s, 1].T
        for c in range(chunks):
            srcc[c, s] = jnp.concatenate([re[c * h:(c + 1) * h], im[c * h:(c + 1) * h]], axis=0)

    for s in range(2):
        loads[1 + s].wait()
        for c in range(chunks):
            st[c, s] = cprod(pre[s, 0], pre[s, 1], srcc[c, s].astype(BF16)).astype(BF16)
            if s == 0:
                @pl.when(me > 0)
                def _():
                    copies[0][c][0].start()

    for s in range(2):
        loads[3 + s].wait()

    def phase1(sweep, c):
        to_prev, to_next = copies[sweep][c]
        hand[sweep, c] = cprod_adj(cpl[1, 0], cpl[1, 1], st[c, 1]).astype(BF16)

        @pl.when(me < n - 1)
        def _():
            to_next.start()

        part[c, 2] = cprod_adj(cpl[0, 0], cpl[0, 1], st[c, 0]).astype(BF16).astype(F32)
        part[c, 1] = local(c, 1)
        part[c, 0] = local(c, 0) + cprod(cpl[0, 0], cpl[0, 1], st[c, 1])

    def phase2(sweep, c):
        to_prev, to_next = copies[sweep][c]

        @pl.when(me > 0)
        def _():
            to_next.wait_recv()

        d0 = (part[c, 0] + arrive[sweep, c].astype(F32)).astype(BF16)

        @pl.when(me > 0)
        def _():
            to_prev.wait_send()

        st[c, 0] = cprod(pre[0, 0], pre[0, 1], d0).astype(BF16)
        if sweep + 1 < sweeps:
            @pl.when(me > 0)
            def _():
                copies[sweep + 1][c][0].start()

        @pl.when(me < n - 1)
        def _():
            to_prev.wait_recv()

        upper = cprod(cpl[1, 0], cpl[1, 1], follow[sweep, c])
        d1 = ((part[c, 1] + upper) + part[c, 2]).astype(BF16)
        st[c, 1] = cprod(pre[1, 0], pre[1, 1], d1).astype(BF16)

        @pl.when(me < n - 1)
        def _():
            to_next.wait_send()

    swaps = [pltpu.make_async_remote_copy(
        src_ref=st.at[c], dst_ref=other.at[c], send_sem=swap_sem.at[0, c],
        recv_sem=swap_sem.at[1, c], device_id=(mate, me), device_id_type=MESH)
        for c in range(chunks)]

    for c in range(chunks):
        phase1(0, c)
    for sweep in range(sweeps):
        for c in range(chunks):
            phase2(sweep, c)
            if sweep + 1 < sweeps:
                phase1(sweep + 1, c)
            else:
                swaps[c].start()

    for c in range(chunks):
        for s in range(2):
            out_ref[0, s, :, c * w:(c + 1) * w] = st[c, s].T
    for c in range(chunks):
        swaps[c].wait()
        for s in range(2):
            out_ref[1, s, :, c * w:(c + 1) * w] = other[c, s].T


def solve(precond, coupling, source, sigma, n):
    m, h = source.shape[-2:]
    chunks = 2
    sweeps = SWEEPS - 1
    blk = (2 * h // chunks, m)
    vmem = pl.BlockSpec(memory_space=pltpu.VMEM)
    anyspace = pl.BlockSpec(memory_space=pl.ANY)
    return pl.pallas_call(
        functools.partial(solve_kernel, n, chunks),
        out_shape=jax.ShapeDtypeStruct((2, 2, m, 2 * h), BF16),
        in_specs=[anyspace, anyspace, anyspace, vmem],
        out_specs=vmem,
        scratch_shapes=[
            pltpu.VMEM(precond.shape[1:], BF16),
            pltpu.VMEM(coupling.shape, BF16),
            pltpu.VMEM(source.shape[1:], F32),
            pltpu.VMEM((chunks, 2) + blk, F32),
            pltpu.VMEM((chunks, 2) + blk, BF16),
            pltpu.VMEM((sweeps, chunks) + blk, BF16),
            pltpu.VMEM((sweeps, chunks) + blk, BF16),
            pltpu.VMEM((sweeps, chunks) + blk, BF16),
            pltpu.VMEM((chunks, 2) + blk, BF16),
            pltpu.VMEM((chunks, 3) + blk, F32),
            pltpu.SemaphoreType.DMA((5,)),
            pltpu.SemaphoreType.DMA((2, sweeps, chunks)),
            pltpu.SemaphoreType.DMA((2, sweeps, chunks)),
            pltpu.SemaphoreType.DMA((2, chunks)),
        ],
        compiler_params=pltpu.CompilerParams(collective_id=0, has_side_effects=True),
    )(precond, coupling, source, sigma)


def self_kernel(both_ref, occ_ref, off_ref, wt_ref, less_ref, great_ref):
    h = both_ref.shape[-1] // 2
    energy_total = occ_ref.shape[0]
    e = lax.axis_index("energy")
    mate = 1 - e
    coef_own = jnp.float32(0.0)
    coef_mate = jnp.float32(0.0)
    for j in range(off_ref.shape[1]):
        t = e + off_ref[e, j]
        inside = jnp.logical_and(t >= 0, t < energy_total)
        w = jnp.where(inside, wt_ref[e, j], jnp.float32(0.0)) / h
        coef_own = coef_own + jnp.where(t == e, w, jnp.float32(0.0))
        coef_mate = coef_mate + jnp.where(t == mate, w, jnp.float32(0.0))
    occ_own = occ_ref[pl.ds(e, 1), :]
    occ_mate = occ_ref[pl.ds(mate, 1), :]
    lanes = lax.broadcasted_iota(jnp.int32, (1, h), 1)
    low = lanes < h // 2
    pos_low = jnp.where(low, 1.0, -1.0).astype(BF16)

    def turn(x):
        return pltpu.roll(x, h // 2, 1)

    def spread(v):
        return jnp.concatenate([jnp.where(low, v, turn(v)), jnp.where(low, turn(v), v)], axis=1)

    scales = []
    for own_part, mate_part in ((occ_own, occ_mate), (1.0 - occ_own, 1.0 - occ_mate)):
        scales.append(jnp.concatenate([spread(coef_own * own_part), spread(coef_mate * mate_part)], axis=1))
    own = both_ref[0, 0]
    mate_states = both_ref[1, 0]
    a = jnp.concatenate([own, mate_states], axis=1)
    blocks = [x[:, i * h:(i + 1) * h] for x in (own, mate_states) for i in range(2)]
    swapped = jnp.concatenate(
        [(turn(b.astype(F32)) * pos_low.astype(F32)).astype(BF16) for b in blocks], axis=1)
    af = a.astype(F32)
    lhs = jnp.concatenate([a, swapped], axis=0)
    m = a.shape[0]
    for scale, out in zip(scales, (less_ref, great_ref)):
        b = (af * scale).astype(BF16)
        both = nt_dot(lhs, b)
        out[0, 0, 0] = both[:m].astype(BF16)
        out[0, 0, 1] = both[m:].astype(BF16)


def self_energy(both, occupation, shift_offsets, shift_weights):
    m, w = both.shape[2:]
    shape = jax.ShapeDtypeStruct((1, 2, 2, m, m), BF16)
    smem = pl.BlockSpec(memory_space=pltpu.SMEM)
    out_spec = pl.BlockSpec((1, 1, 2, m, m), lambda s: (0, s, 0, 0, 0))
    return pl.pallas_call(
        self_kernel,
        out_shape=(shape, shape),
        grid=(2,),
        in_specs=[
            pl.BlockSpec((2, 1, m, w), lambda s: (0, s, 0, 0)),
            pl.BlockSpec(occupation.shape, lambda s: (0, 0)),
            smem,
            smem,
        ],
        out_specs=(out_spec, out_spec),
    )(both, occupation, shift_offsets, shift_weights)


def body(precond, coupling, source, sigma_ret, occupation, shift_offsets, shift_weights):
    n = lax.axis_size("space")
    both = solve(precond, coupling, source, sigma_ret, n)
    return self_energy(both, occupation, shift_offsets, shift_weights)


def solution(mesh):
    placed = (
        P("energy", "space", None, None, None),
        P("space", None, None, None),
        P("energy", "space", None, None, None),
        P("energy", "space", None, None),
        P(),
        P(),
        P(),
    )
    return jax.shard_map(
        body,
        mesh=mesh,
        in_specs=placed,
        out_specs=(P("energy", "space", None, None, None), P("energy", "space", None, None, None)),
        check_vma=False,
    )
```

```python
import functools

import jax
import jax.numpy as jnp
from jax import lax
from jax.experimental import pallas as pl
from jax.experimental.pallas import tpu as pltpu
from jax.sharding import PartitionSpec as P

SWEEPS = 4
MESH = pl.DeviceIdType.MESH
F32 = jnp.float32
BF16 = jnp.bfloat16


def dot(a, b):
    return jnp.dot(a, b, preferred_element_type=F32)


def nt_dot(a, b):
    return lax.dot_general(a, b, (((1,), (1,)), ((), ())), preferred_element_type=F32)


def solve_kernel(n, chunks, pre_hbm, cpl_hbm, src_hbm, sig_ref, out_ref,
                 pre, cpl, src, srcc, st, follow, arrive, hand, other, part,
                 load_sem, send_sem, recv_sem, swap_sem):
    me = lax.axis_index("space")
    en = lax.axis_index("energy")
    prev = lax.rem(me + n - 1, n)
    nxt = lax.rem(me + 1, n)
    mate = 1 - en
    w = st.shape[-2]
    h = w // 2

    loads = [pltpu.make_async_copy(src_hbm.at[0], src, load_sem.at[0])]
    loads += [pltpu.make_async_copy(pre_hbm.at[0, s], pre.at[s], load_sem.at[1 + s]) for s in range(2)]
    loads += [pltpu.make_async_copy(cpl_hbm.at[s], cpl.at[s], load_sem.at[3 + s]) for s in range(2)]
    for c in loads:
        c.start()

    barrier = pltpu.get_barrier_semaphore()
    for peer in ((en, prev), (en, nxt), (mate, me)):
        pl.semaphore_signal(barrier, inc=1, device_id=peer, device_id_type=MESH)
    pl.semaphore_wait(barrier, 3)

    @pl.when(me == n - 1)
    def _():
        follow[...] = jnp.zeros_like(follow)

    @pl.when(me == 0)
    def _():
        arrive[...] = jnp.zeros_like(arrive)

    def cprod(mr, mi, rhs):
        x = nt_dot(rhs, mr)
        y = nt_dot(rhs, mi)
        return jnp.concatenate([x[:h] - y[h:], x[h:] + y[:h]], axis=0)

    def cprod_adj(mr, mi, rhs):
        x = dot(rhs, mr)
        y = dot(rhs, mi)
        return jnp.concatenate([x[:h] + y[h:], x[h:] - y[:h]], axis=0)

    def local(c, s):
        x = st[c, s].astype(F32)
        xr, xi = x[:h], x[h:]
        gr = sig_ref[0, s, pl.ds(0, 1), :]
        gi = sig_ref[0, s, pl.ds(1, 1), :]
        return srcc[c, s] + jnp.concatenate([gr * xr - gi * xi, gr * xi + gi * xr], axis=0)

    sweeps = SWEEPS - 1

    def sends(sweep, c):
        to_prev = pltpu.make_async_remote_copy(
            src_ref=st.at[c, 0], dst_ref=follow.at[sweep, c],
            send_sem=send_sem.at[0, sweep, c], recv_sem=recv_sem.at[0, sweep, c],
            device_id=(en, prev), device_id_type=MESH)
        to_next = pltpu.make_async_remote_copy(
            src_ref=hand.at[sweep, c], dst_ref=arrive.at[sweep, c],
            send_sem=send_sem.at[1, sweep, c], recv_sem=recv_sem.at[1, sweep, c],
            device_id=(en, nxt), device_id_type=MESH)
        return to_prev, to_next

    copies = [[sends(sweep, c) for c in range(chunks)] for sweep in range(sweeps)]

    loads[0].wait()
    for s in range(2):
        re = src[s, 0].T
        im = src[s, 1].T
        for c in range(chunks):
            srcc[c, s] = jnp.concatenate([re[c * h:(c + 1) * h], im[c * h:(c + 1) * h]], axis=0)

    for s in range(2):
        loads[1 + s].wait()
        rhs = jnp.concatenate([srcc[c, s] for c in range(chunks)], axis=0).astype(BF16)
        x = nt_dot(rhs, pre[s, 0])
        y = nt_dot(rhs, pre[s, 1])
        for c in range(chunks):
            lo, mid, hi = c * w, c * w + h, (c + 1) * w
            st[c, s] = jnp.concatenate(
                [x[lo:mid] - y[mid:hi], x[mid:hi] + y[lo:mid]], axis=0).astype(BF16)
            if s == 0:
                @pl.when(me > 0)
                def _():
                    copies[0][c][0].start()

    for s in range(2):
        loads[3 + s].wait()

    def phase1(sweep, c):
        to_prev, to_next = copies[sweep][c]
        hand[sweep, c] = cprod_adj(cpl[1, 0], cpl[1, 1], st[c, 1]).astype(BF16)

        @pl.when(me < n - 1)
        def _():
            to_next.start()

        part[c, 2] = cprod_adj(cpl[0, 0], cpl[0, 1], st[c, 0]).astype(BF16).astype(F32)
        part[c, 1] = local(c, 1)
        part[c, 0] = local(c, 0) + cprod(cpl[0, 0], cpl[0, 1], st[c, 1])

    def phase2(sweep, c):
        to_prev, to_next = copies[sweep][c]

        @pl.when(me > 0)
        def _():
            to_next.wait_recv()

        d0 = (part[c, 0] + arrive[sweep, c].astype(F32)).astype(BF16)

        @pl.when(me > 0)
        def _():
            to_prev.wait_send()

        st[c, 0] = cprod(pre[0, 0], pre[0, 1], d0).astype(BF16)
        if sweep + 1 < sweeps:
            @pl.when(me > 0)
            def _():
                copies[sweep + 1][c][0].start()

        @pl.when(me < n - 1)
        def _():
            to_prev.wait_recv()

        upper = cprod(cpl[1, 0], cpl[1, 1], follow[sweep, c])
        d1 = ((part[c, 1] + upper) + part[c, 2]).astype(BF16)
        st[c, 1] = cprod(pre[1, 0], pre[1, 1], d1).astype(BF16)

        @pl.when(me < n - 1)
        def _():
            to_next.wait_send()

    swaps = [pltpu.make_async_remote_copy(
        src_ref=st.at[c], dst_ref=other.at[c], send_sem=swap_sem.at[0, c],
        recv_sem=swap_sem.at[1, c], device_id=(mate, me), device_id_type=MESH)
        for c in range(chunks)]

    for c in range(chunks):
        phase1(0, c)
    for sweep in range(sweeps):
        for c in range(chunks):
            phase2(sweep, c)
            if sweep + 1 < sweeps:
                phase1(sweep + 1, c)
            else:
                swaps[c].start()

    for c in range(chunks):
        for s in range(2):
            out_ref[0, s, :, c * w:(c + 1) * w] = st[c, s].T
    for c in range(chunks):
        swaps[c].wait()
        for s in range(2):
            out_ref[1, s, :, c * w:(c + 1) * w] = other[c, s].T


def solve(precond, coupling, source, sigma, n):
    m, h = source.shape[-2:]
    chunks = 2
    sweeps = SWEEPS - 1
    blk = (2 * h // chunks, m)
    vmem = pl.BlockSpec(memory_space=pltpu.VMEM)
    anyspace = pl.BlockSpec(memory_space=pl.ANY)
    return pl.pallas_call(
        functools.partial(solve_kernel, n, chunks),
        out_shape=jax.ShapeDtypeStruct((2, 2, m, 2 * h), BF16),
        in_specs=[anyspace, anyspace, anyspace, vmem],
        out_specs=vmem,
        scratch_shapes=[
            pltpu.VMEM(precond.shape[1:], BF16),
            pltpu.VMEM(coupling.shape, BF16),
            pltpu.VMEM(source.shape[1:], F32),
            pltpu.VMEM((chunks, 2) + blk, F32),
            pltpu.VMEM((chunks, 2) + blk, BF16),
            pltpu.VMEM((sweeps, chunks) + blk, BF16),
            pltpu.VMEM((sweeps, chunks) + blk, BF16),
            pltpu.VMEM((sweeps, chunks) + blk, BF16),
            pltpu.VMEM((chunks, 2) + blk, BF16),
            pltpu.VMEM((chunks, 3) + blk, F32),
            pltpu.SemaphoreType.DMA((5,)),
            pltpu.SemaphoreType.DMA((2, sweeps, chunks)),
            pltpu.SemaphoreType.DMA((2, sweeps, chunks)),
            pltpu.SemaphoreType.DMA((2, chunks)),
        ],
        compiler_params=pltpu.CompilerParams(collective_id=0, has_side_effects=True),
    )(precond, coupling, source, sigma)


def self_kernel(both_ref, occ_ref, off_ref, wt_ref, less_ref, great_ref):
    h = both_ref.shape[-1] // 2
    energy_total = occ_ref.shape[0]
    e = lax.axis_index("energy")
    mate = 1 - e
    coef_own = jnp.float32(0.0)
    coef_mate = jnp.float32(0.0)
    for j in range(off_ref.shape[1]):
        t = e + off_ref[e, j]
        inside = jnp.logical_and(t >= 0, t < energy_total)
        w = jnp.where(inside, wt_ref[e, j], jnp.float32(0.0)) / h
        coef_own = coef_own + jnp.where(t == e, w, jnp.float32(0.0))
        coef_mate = coef_mate + jnp.where(t == mate, w, jnp.float32(0.0))
    occ_own = occ_ref[pl.ds(e, 1), :]
    occ_mate = occ_ref[pl.ds(mate, 1), :]
    lanes = lax.broadcasted_iota(jnp.int32, (1, h), 1)
    low = lanes < h // 2
    pos_low = jnp.where(low, 1.0, -1.0).astype(BF16)

    def turn(x):
        return pltpu.roll(x, h // 2, 1)

    def spread(v):
        return jnp.concatenate([jnp.where(low, v, turn(v)), jnp.where(low, turn(v), v)], axis=1)

    scales = []
    for own_part, mate_part in ((occ_own, occ_mate), (1.0 - occ_own, 1.0 - occ_mate)):
        scales.append(jnp.concatenate([spread(coef_own * own_part), spread(coef_mate * mate_part)], axis=1))
    own = both_ref[0, 0]
    mate_states = both_ref[1, 0]
    a = jnp.concatenate([own, mate_states], axis=1)
    blocks = [x[:, i * h:(i + 1) * h] for x in (own, mate_states) for i in range(2)]
    swapped = jnp.concatenate(
        [(turn(b.astype(F32)) * pos_low.astype(F32)).astype(BF16) for b in blocks], axis=1)
    af = a.astype(F32)
    lhs = jnp.concatenate([a, swapped], axis=0)
    m = a.shape[0]
    for scale, out in zip(scales, (less_ref, great_ref)):
        b = (af * scale).astype(BF16)
        both = nt_dot(lhs, b)
        out[0, 0, 0] = both[:m].astype(BF16)
        out[0, 0, 1] = both[m:].astype(BF16)


def self_energy(both, occupation, shift_offsets, shift_weights):
    m, w = both.shape[2:]
    shape = jax.ShapeDtypeStruct((1, 2, 2, m, m), BF16)
    smem = pl.BlockSpec(memory_space=pltpu.SMEM)
    out_spec = pl.BlockSpec((1, 1, 2, m, m), lambda s: (0, s, 0, 0, 0))
    return pl.pallas_call(
        self_kernel,
        out_shape=(shape, shape),
        grid=(2,),
        in_specs=[
            pl.BlockSpec((2, 1, m, w), lambda s: (0, s, 0, 0)),
            pl.BlockSpec(occupation.shape, lambda s: (0, 0)),
            smem,
            smem,
        ],
        out_specs=(out_spec, out_spec),
    )(both, occupation, shift_offsets, shift_weights)


def body(precond, coupling, source, sigma_ret, occupation, shift_offsets, shift_weights):
    n = lax.axis_size("space")
    both = solve(precond, coupling, source, sigma_ret, n)
    return self_energy(both, occupation, shift_offsets, shift_weights)


def solution(mesh):
    placed = (
        P("energy", "space", None, None, None),
        P("space", None, None, None),
        P("energy", "space", None, None, None),
        P("energy", "space", None, None),
        P(),
        P(),
        P(),
    )
    return jax.shard_map(
        body,
        mesh=mesh,
        in_specs=placed,
        out_specs=(P("energy", "space", None, None, None), P("energy", "space", None, None, None)),
        check_vma=False,
    )
```

```python
import functools

import jax
import jax.numpy as jnp
from jax import lax
from jax.experimental import pallas as pl
from jax.experimental.pallas import tpu as pltpu
from jax.sharding import PartitionSpec as P

SWEEPS = 4
MESH = pl.DeviceIdType.MESH
F32 = jnp.float32
BF16 = jnp.bfloat16


def dot(a, b):
    return jnp.dot(a, b, preferred_element_type=F32)


def nt_dot(a, b):
    return lax.dot_general(a, b, (((1,), (1,)), ((), ())), preferred_element_type=F32)


def solve_kernel(n, chunks, pre_hbm, cpl_hbm, src_hbm, sig_ref, out_ref,
                 pre, cpl, src, srcc, st, follow, arrive, hand, other, part,
                 load_sem, send_sem, recv_sem, swap_sem):
    me = lax.axis_index("space")
    en = lax.axis_index("energy")
    prev = lax.rem(me + n - 1, n)
    nxt = lax.rem(me + 1, n)
    mate = 1 - en
    w = st.shape[-2]
    h = w // 2

    loads = [pltpu.make_async_copy(src_hbm.at[0], src, load_sem.at[0])]
    loads += [pltpu.make_async_copy(pre_hbm.at[0, s], pre.at[s], load_sem.at[1 + s]) for s in range(2)]
    loads += [pltpu.make_async_copy(cpl_hbm.at[s], cpl.at[s], load_sem.at[3 + s]) for s in range(2)]
    for c in loads:
        c.start()

    barrier = pltpu.get_barrier_semaphore()
    for peer in ((en, prev), (en, nxt), (mate, me)):
        pl.semaphore_signal(barrier, inc=1, device_id=peer, device_id_type=MESH)
    pl.semaphore_wait(barrier, 3)

    @pl.when(me == n - 1)
    def _():
        follow[...] = jnp.zeros_like(follow)

    @pl.when(me == 0)
    def _():
        arrive[...] = jnp.zeros_like(arrive)

    def cprod(mr, mi, rhs):
        x = nt_dot(rhs, mr)
        y = nt_dot(rhs, mi)
        return jnp.concatenate([x[:h] - y[h:], x[h:] + y[:h]], axis=0)

    def cprod_adj(mr, mi, rhs):
        x = dot(rhs, mr)
        y = dot(rhs, mi)
        return jnp.concatenate([x[:h] + y[h:], x[h:] - y[:h]], axis=0)

    def local(c, s):
        x = st[c, s].astype(F32)
        xr, xi = x[:h], x[h:]
        gr = sig_ref[0, s, pl.ds(0, 1), :]
        gi = sig_ref[0, s, pl.ds(1, 1), :]
        return srcc[c, s] + jnp.concatenate([gr * xr - gi * xi, gr * xi + gi * xr], axis=0)

    sweeps = SWEEPS - 1

    def sends(sweep, c):
        to_prev = pltpu.make_async_remote_copy(
            src_ref=st.at[c, 0], dst_ref=follow.at[sweep, c],
            send_sem=send_sem.at[0, sweep, c], recv_sem=recv_sem.at[0, sweep, c],
            device_id=(en, prev), device_id_type=MESH)
        to_next = pltpu.make_async_remote_copy(
            src_ref=hand.at[sweep, c], dst_ref=arrive.at[sweep, c],
            send_sem=send_sem.at[1, sweep, c], recv_sem=recv_sem.at[1, sweep, c],
            device_id=(en, nxt), device_id_type=MESH)
        return to_prev, to_next

    copies = [[sends(sweep, c) for c in range(chunks)] for sweep in range(sweeps)]

    loads[0].wait()
    for s in range(2):
        re = src[s, 0].T
        im = src[s, 1].T
        for c in range(chunks):
            srcc[c, s] = jnp.concatenate([re[c * h:(c + 1) * h], im[c * h:(c + 1) * h]], axis=0)

    for s in range(2):
        loads[1 + s].wait()
        rhs = jnp.concatenate([srcc[c, s] for c in range(chunks)], axis=0).astype(BF16)
        x = nt_dot(rhs, pre[s, 0])
        y = nt_dot(rhs, pre[s, 1])
        for c in range(chunks):
            lo, mid, hi = c * w, c * w + h, (c + 1) * w
            st[c, s] = jnp.concatenate(
                [x[lo:mid] - y[mid:hi], x[mid:hi] + y[lo:mid]], axis=0).astype(BF16)
            if s == 0:
                @pl.when(me > 0)
                def _():
                    copies[0][c][0].start()

    for s in range(2):
        loads[3 + s].wait()

    def phase1(sweep, c):
        to_prev, to_next = copies[sweep][c]
        hand[sweep, c] = cprod_adj(cpl[1, 0], cpl[1, 1], st[c, 1]).astype(BF16)

        @pl.when(me < n - 1)
        def _():
            to_next.start()

        part[c, 2] = cprod_adj(cpl[0, 0], cpl[0, 1], st[c, 0]).astype(BF16).astype(F32)
        part[c, 1] = local(c, 1)
        part[c, 0] = local(c, 0) + cprod(cpl[0, 0], cpl[0, 1], st[c, 1])

    def phase2(sweep, c):
        to_prev, to_next = copies[sweep][c]

        @pl.when(me > 0)
        def _():
            to_next.wait_recv()

        d0 = (part[c, 0] + arrive[sweep, c].astype(F32)).astype(BF16)

        @pl.when(me > 0)
        def _():
            to_prev.wait_send()

        st[c, 0] = cprod(pre[0, 0], pre[0, 1], d0).astype(BF16)
        if sweep + 1 < sweeps:
            @pl.when(me > 0)
            def _():
                copies[sweep + 1][c][0].start()

        @pl.when(me < n - 1)
        def _():
            to_prev.wait_recv()

        upper = cprod(cpl[1, 0], cpl[1, 1], follow[sweep, c])
        d1 = ((part[c, 1] + upper) + part[c, 2]).astype(BF16)
        st[c, 1] = cprod(pre[1, 0], pre[1, 1], d1).astype(BF16)

        @pl.when(me < n - 1)
        def _():
            to_next.wait_send()

    swaps = [pltpu.make_async_remote_copy(
        src_ref=st.at[c], dst_ref=other.at[c], send_sem=swap_sem.at[0, c],
        recv_sem=swap_sem.at[1, c], device_id=(mate, me), device_id_type=MESH)
        for c in range(chunks)]

    def both_rows(c, x, y, sign):
        lo, mid, hi = c * w, c * w + h, (c + 1) * w
        return jnp.concatenate([x[lo:mid] - sign * y[mid:hi], x[mid:hi] + sign * y[lo:mid]], axis=0)

    rows1 = jnp.concatenate([st[c, 1] for c in range(chunks)], axis=0)
    rows0 = jnp.concatenate([st[c, 0] for c in range(chunks)], axis=0)
    hx = dot(rows1, cpl[1, 0])
    hy = dot(rows1, cpl[1, 1])
    for c in range(chunks):
        hand[0, c] = both_rows(c, hx, hy, -1.0).astype(BF16)

        @pl.when(me < n - 1)
        def _():
            copies[0][c][1].start()

    lx = dot(rows0, cpl[0, 0])
    ly = dot(rows0, cpl[0, 1])
    ux = nt_dot(rows1, cpl[0, 0])
    uy = nt_dot(rows1, cpl[0, 1])
    for c in range(chunks):
        part[c, 2] = both_rows(c, lx, ly, -1.0).astype(BF16).astype(F32)
        part[c, 1] = local(c, 1)
        part[c, 0] = local(c, 0) + both_rows(c, ux, uy, 1.0)
    for sweep in range(sweeps):
        for c in range(chunks):
            phase2(sweep, c)
            if sweep + 1 < sweeps:
                phase1(sweep + 1, c)
            else:
                swaps[c].start()

    for c in range(chunks):
        for s in range(2):
            out_ref[0, s, :, c * w:(c + 1) * w] = st[c, s].T
    for c in range(chunks):
        swaps[c].wait()
        for s in range(2):
            out_ref[1, s, :, c * w:(c + 1) * w] = other[c, s].T


def solve(precond, coupling, source, sigma, n):
    m, h = source.shape[-2:]
    chunks = 2
    sweeps = SWEEPS - 1
    blk = (2 * h // chunks, m)
    vmem = pl.BlockSpec(memory_space=pltpu.VMEM)
    anyspace = pl.BlockSpec(memory_space=pl.ANY)
    return pl.pallas_call(
        functools.partial(solve_kernel, n, chunks),
        out_shape=jax.ShapeDtypeStruct((2, 2, m, 2 * h), BF16),
        in_specs=[anyspace, anyspace, anyspace, vmem],
        out_specs=vmem,
        scratch_shapes=[
            pltpu.VMEM(precond.shape[1:], BF16),
            pltpu.VMEM(coupling.shape, BF16),
            pltpu.VMEM(source.shape[1:], F32),
            pltpu.VMEM((chunks, 2) + blk, F32),
            pltpu.VMEM((chunks, 2) + blk, BF16),
            pltpu.VMEM((sweeps, chunks) + blk, BF16),
            pltpu.VMEM((sweeps, chunks) + blk, BF16),
            pltpu.VMEM((sweeps, chunks) + blk, BF16),
            pltpu.VMEM((chunks, 2) + blk, BF16),
            pltpu.VMEM((chunks, 3) + blk, F32),
            pltpu.SemaphoreType.DMA((5,)),
            pltpu.SemaphoreType.DMA((2, sweeps, chunks)),
            pltpu.SemaphoreType.DMA((2, sweeps, chunks)),
            pltpu.SemaphoreType.DMA((2, chunks)),
        ],
        compiler_params=pltpu.CompilerParams(collective_id=0, has_side_effects=True),
    )(precond, coupling, source, sigma)


def self_kernel(both_ref, occ_ref, off_ref, wt_ref, less_ref, great_ref):
    h = both_ref.shape[-1] // 2
    energy_total = occ_ref.shape[0]
    e = lax.axis_index("energy")
    mate = 1 - e
    coef_own = jnp.float32(0.0)
    coef_mate = jnp.float32(0.0)
    for j in range(off_ref.shape[1]):
        t = e + off_ref[e, j]
        inside = jnp.logical_and(t >= 0, t < energy_total)
        w = jnp.where(inside, wt_ref[e, j], jnp.float32(0.0)) / h
        coef_own = coef_own + jnp.where(t == e, w, jnp.float32(0.0))
        coef_mate = coef_mate + jnp.where(t == mate, w, jnp.float32(0.0))
    occ_own = occ_ref[pl.ds(e, 1), :]
    occ_mate = occ_ref[pl.ds(mate, 1), :]
    lanes = lax.broadcasted_iota(jnp.int32, (1, h), 1)
    low = lanes < h // 2
    pos_low = jnp.where(low, 1.0, -1.0).astype(BF16)

    def turn(x):
        return pltpu.roll(x, h // 2, 1)

    def spread(v):
        return jnp.concatenate([jnp.where(low, v, turn(v)), jnp.where(low, turn(v), v)], axis=1)

    scales = []
    for own_part, mate_part in ((occ_own, occ_mate), (1.0 - occ_own, 1.0 - occ_mate)):
        scales.append(jnp.concatenate([spread(coef_own * own_part), spread(coef_mate * mate_part)], axis=1))
    own = both_ref[0, 0]
    mate_states = both_ref[1, 0]
    a = jnp.concatenate([own, mate_states], axis=1)
    blocks = [x[:, i * h:(i + 1) * h] for x in (own, mate_states) for i in range(2)]
    swapped = jnp.concatenate(
        [(turn(b.astype(F32)) * pos_low.astype(F32)).astype(BF16) for b in blocks], axis=1)
    af = a.astype(F32)
    lhs = jnp.concatenate([a, swapped], axis=0)
    m = a.shape[0]
    for scale, out in zip(scales, (less_ref, great_ref)):
        b = (af * scale).astype(BF16)
        both = nt_dot(lhs, b)
        out[0, 0, 0] = both[:m].astype(BF16)
        out[0, 0, 1] = both[m:].astype(BF16)


def self_energy(both, occupation, shift_offsets, shift_weights):
    m, w = both.shape[2:]
    shape = jax.ShapeDtypeStruct((1, 2, 2, m, m), BF16)
    smem = pl.BlockSpec(memory_space=pltpu.SMEM)
    out_spec = pl.BlockSpec((1, 1, 2, m, m), lambda s: (0, s, 0, 0, 0))
    return pl.pallas_call(
        self_kernel,
        out_shape=(shape, shape),
        grid=(2,),
        in_specs=[
            pl.BlockSpec((2, 1, m, w), lambda s: (0, s, 0, 0)),
            pl.BlockSpec(occupation.shape, lambda s: (0, 0)),
            smem,
            smem,
        ],
        out_specs=(out_spec, out_spec),
    )(both, occupation, shift_offsets, shift_weights)


def body(precond, coupling, source, sigma_ret, occupation, shift_offsets, shift_weights):
    n = lax.axis_size("space")
    both = solve(precond, coupling, source, sigma_ret, n)
    return self_energy(both, occupation, shift_offsets, shift_weights)


def solution(mesh):
    placed = (
        P("energy", "space", None, None, None),
        P("space", None, None, None),
        P("energy", "space", None, None, None),
        P("energy", "space", None, None),
        P(),
        P(),
        P(),
    )
    return jax.shard_map(
        body,
        mesh=mesh,
        in_specs=placed,
        out_specs=(P("energy", "space", None, None, None), P("energy", "space", None, None, None)),
        check_vma=False,
    )
```

```python
import functools

import jax
import jax.numpy as jnp
from jax import lax
from jax.experimental import pallas as pl
from jax.experimental.pallas import tpu as pltpu
from jax.sharding import PartitionSpec as P

SWEEPS = 4
MESH = pl.DeviceIdType.MESH
F32 = jnp.float32
BF16 = jnp.bfloat16


def dot(a, b):
    return jnp.dot(a, b, preferred_element_type=F32)


def nt_dot(a, b):
    return lax.dot_general(a, b, (((1,), (1,)), ((), ())), preferred_element_type=F32)


def solve_kernel(n, chunks, pre_hbm, cpl_hbm, src_hbm, sig_ref, out_ref,
                 pre, cpl, src, srcc, st, follow, arrive, hand, other, part,
                 load_sem, send_sem, recv_sem, swap_sem):
    me = lax.axis_index("space")
    en = lax.axis_index("energy")
    prev = lax.rem(me + n - 1, n)
    nxt = lax.rem(me + 1, n)
    mate = 1 - en
    w = st.shape[-2]
    h = w // 2

    loads = [pltpu.make_async_copy(src_hbm.at[0], src, load_sem.at[0])]
    loads += [pltpu.make_async_copy(pre_hbm.at[0, s], pre.at[s], load_sem.at[1 + s]) for s in range(2)]
    loads += [pltpu.make_async_copy(cpl_hbm.at[s], cpl.at[s], load_sem.at[3 + s]) for s in range(2)]
    for c in loads:
        c.start()

    barrier = pltpu.get_barrier_semaphore()
    for peer in ((en, prev), (en, nxt), (mate, me)):
        pl.semaphore_signal(barrier, inc=1, device_id=peer, device_id_type=MESH)
    pl.semaphore_wait(barrier, 3)

    @pl.when(me == n - 1)
    def _():
        follow[...] = jnp.zeros_like(follow)

    @pl.when(me == 0)
    def _():
        arrive[...] = jnp.zeros_like(arrive)

    def cprod(mr, mi, rhs):
        x = nt_dot(rhs, mr)
        y = nt_dot(rhs, mi)
        return jnp.concatenate([x[:h] - y[h:], x[h:] + y[:h]], axis=0)

    def cprod_adj(mr, mi, rhs):
        x = dot(rhs, mr)
        y = dot(rhs, mi)
        return jnp.concatenate([x[:h] + y[h:], x[h:] - y[:h]], axis=0)

    def local(c, s):
        x = st[c, s].astype(F32)
        xr, xi = x[:h], x[h:]
        gr = sig_ref[0, s, pl.ds(0, 1), :]
        gi = sig_ref[0, s, pl.ds(1, 1), :]
        return srcc[c, s] + jnp.concatenate([gr * xr - gi * xi, gr * xi + gi * xr], axis=0)

    sweeps = SWEEPS - 1

    def sends(sweep, c):
        to_prev = pltpu.make_async_remote_copy(
            src_ref=st.at[c, 0], dst_ref=follow.at[sweep, c],
            send_sem=send_sem.at[0, sweep, c], recv_sem=recv_sem.at[0, sweep, c],
            device_id=(en, prev), device_id_type=MESH)
        to_next = pltpu.make_async_remote_copy(
            src_ref=hand.at[sweep, c], dst_ref=arrive.at[sweep, c],
            send_sem=send_sem.at[1, sweep, c], recv_sem=recv_sem.at[1, sweep, c],
            device_id=(en, nxt), device_id_type=MESH)
        return to_prev, to_next

    copies = [[sends(sweep, c) for c in range(chunks)] for sweep in range(sweeps)]

    loads[0].wait()
    for s in range(2):
        re = src[s, 0].T
        im = src[s, 1].T
        for c in range(chunks):
            srcc[c, s] = jnp.concatenate([re[c * h:(c + 1) * h], im[c * h:(c + 1) * h]], axis=0)

    for s in range(2):
        loads[1 + s].wait()
        rhs = jnp.concatenate([srcc[c, s] for c in range(chunks)], axis=0).astype(BF16)
        x = nt_dot(rhs, pre[s, 0])
        y = nt_dot(rhs, pre[s, 1])
        for c in range(chunks):
            lo, mid, hi = c * w, c * w + h, (c + 1) * w
            st[c, s] = jnp.concatenate(
                [x[lo:mid] - y[mid:hi], x[mid:hi] + y[lo:mid]], axis=0).astype(BF16)
            if s == 0:
                @pl.when(me > 0)
                def _():
                    copies[0][c][0].start()

    for s in range(2):
        loads[3 + s].wait()

    def phase1(sweep, c):
        to_prev, to_next = copies[sweep][c]
        hand[sweep, c] = cprod_adj(cpl[1, 0], cpl[1, 1], st[c, 1]).astype(BF16)

        @pl.when(me < n - 1)
        def _():
            to_next.start()

        part[c, 2] = cprod_adj(cpl[0, 0], cpl[0, 1], st[c, 0]).astype(BF16).astype(F32)
        part[c, 1] = local(c, 1)
        part[c, 0] = local(c, 0) + cprod(cpl[0, 0], cpl[0, 1], st[c, 1])

    def phase2(sweep, c):
        to_prev, to_next = copies[sweep][c]

        @pl.when(me > 0)
        def _():
            to_next.wait_recv()

        d0 = (part[c, 0] + arrive[sweep, c].astype(F32)).astype(BF16)

        @pl.when(me > 0)
        def _():
            to_prev.wait_send()

        st[c, 0] = cprod(pre[0, 0], pre[0, 1], d0).astype(BF16)
        if sweep + 1 < sweeps:
            @pl.when(me > 0)
            def _():
                copies[sweep + 1][c][0].start()

        @pl.when(me < n - 1)
        def _():
            to_prev.wait_recv()

        upper = cprod(cpl[1, 0], cpl[1, 1], follow[sweep, c])
        d1 = ((part[c, 1] + upper) + part[c, 2]).astype(BF16)
        st[c, 1] = cprod(pre[1, 0], pre[1, 1], d1).astype(BF16)

        @pl.when(me < n - 1)
        def _():
            to_next.wait_send()

    swaps = [pltpu.make_async_remote_copy(
        src_ref=st.at[c], dst_ref=other.at[c], send_sem=swap_sem.at[0, c],
        recv_sem=swap_sem.at[1, c], device_id=(mate, me), device_id_type=MESH)
        for c in range(chunks)]

    for c in range(chunks):
        phase1(0, c)
    for sweep in range(sweeps):
        for c in range(chunks):
            phase2(sweep, c)
            if sweep + 1 < sweeps:
                phase1(sweep + 1, c)
            else:
                swaps[c].start()
                for s in range(2):
                    out_ref[0, s, :, c * w:(c + 1) * w] = st[c, s].T

    for c in range(chunks):
        swaps[c].wait()
        for s in range(2):
            out_ref[1, s, :, c * w:(c + 1) * w] = other[c, s].T


def solve(precond, coupling, source, sigma, n):
    m, h = source.shape[-2:]
    chunks = 2
    sweeps = SWEEPS - 1
    blk = (2 * h // chunks, m)
    vmem = pl.BlockSpec(memory_space=pltpu.VMEM)
    anyspace = pl.BlockSpec(memory_space=pl.ANY)
    return pl.pallas_call(
        functools.partial(solve_kernel, n, chunks),
        out_shape=jax.ShapeDtypeStruct((2, 2, m, 2 * h), BF16),
        in_specs=[anyspace, anyspace, anyspace, vmem],
        out_specs=vmem,
        scratch_shapes=[
            pltpu.VMEM(precond.shape[1:], BF16),
            pltpu.VMEM(coupling.shape, BF16),
            pltpu.VMEM(source.shape[1:], F32),
            pltpu.VMEM((chunks, 2) + blk, F32),
            pltpu.VMEM((chunks, 2) + blk, BF16),
            pltpu.VMEM((sweeps, chunks) + blk, BF16),
            pltpu.VMEM((sweeps, chunks) + blk, BF16),
            pltpu.VMEM((sweeps, chunks) + blk, BF16),
            pltpu.VMEM((chunks, 2) + blk, BF16),
            pltpu.VMEM((chunks, 3) + blk, F32),
            pltpu.SemaphoreType.DMA((5,)),
            pltpu.SemaphoreType.DMA((2, sweeps, chunks)),
            pltpu.SemaphoreType.DMA((2, sweeps, chunks)),
            pltpu.SemaphoreType.DMA((2, chunks)),
        ],
        compiler_params=pltpu.CompilerParams(collective_id=0, has_side_effects=True),
    )(precond, coupling, source, sigma)


def self_kernel(both_ref, occ_ref, off_ref, wt_ref, less_ref, great_ref):
    h = both_ref.shape[-1] // 2
    energy_total = occ_ref.shape[0]
    e = lax.axis_index("energy")
    mate = 1 - e
    coef_own = jnp.float32(0.0)
    coef_mate = jnp.float32(0.0)
    for j in range(off_ref.shape[1]):
        t = e + off_ref[e, j]
        inside = jnp.logical_and(t >= 0, t < energy_total)
        w = jnp.where(inside, wt_ref[e, j], jnp.float32(0.0)) / h
        coef_own = coef_own + jnp.where(t == e, w, jnp.float32(0.0))
        coef_mate = coef_mate + jnp.where(t == mate, w, jnp.float32(0.0))
    occ_own = occ_ref[pl.ds(e, 1), :]
    occ_mate = occ_ref[pl.ds(mate, 1), :]
    lanes = lax.broadcasted_iota(jnp.int32, (1, h), 1)
    low = lanes < h // 2
    pos_low = jnp.where(low, 1.0, -1.0).astype(BF16)

    def turn(x):
        return pltpu.roll(x, h // 2, 1)

    def spread(v):
        return jnp.concatenate([jnp.where(low, v, turn(v)), jnp.where(low, turn(v), v)], axis=1)

    scales = []
    for own_part, mate_part in ((occ_own, occ_mate), (1.0 - occ_own, 1.0 - occ_mate)):
        scales.append(jnp.concatenate([spread(coef_own * own_part), spread(coef_mate * mate_part)], axis=1))
    own = both_ref[0, 0]
    mate_states = both_ref[1, 0]
    a = jnp.concatenate([own, mate_states], axis=1)
    blocks = [x[:, i * h:(i + 1) * h] for x in (own, mate_states) for i in range(2)]
    swapped = jnp.concatenate(
        [(turn(b.astype(F32)) * pos_low.astype(F32)).astype(BF16) for b in blocks], axis=1)
    af = a.astype(F32)
    lhs = jnp.concatenate([a, swapped], axis=0)
    m = a.shape[0]
    for scale, out in zip(scales, (less_ref, great_ref)):
        b = (af * scale).astype(BF16)
        both = nt_dot(lhs, b)
        out[0, 0, 0] = both[:m].astype(BF16)
        out[0, 0, 1] = both[m:].astype(BF16)


def self_energy(both, occupation, shift_offsets, shift_weights):
    m, w = both.shape[2:]
    shape = jax.ShapeDtypeStruct((1, 2, 2, m, m), BF16)
    smem = pl.BlockSpec(memory_space=pltpu.SMEM)
    out_spec = pl.BlockSpec((1, 1, 2, m, m), lambda s: (0, s, 0, 0, 0))
    return pl.pallas_call(
        self_kernel,
        out_shape=(shape, shape),
        grid=(2,),
        in_specs=[
            pl.BlockSpec((2, 1, m, w), lambda s: (0, s, 0, 0)),
            pl.BlockSpec(occupation.shape, lambda s: (0, 0)),
            smem,
            smem,
        ],
        out_specs=(out_spec, out_spec),
    )(both, occupation, shift_offsets, shift_weights)


def body(precond, coupling, source, sigma_ret, occupation, shift_offsets, shift_weights):
    n = lax.axis_size("space")
    both = solve(precond, coupling, source, sigma_ret, n)
    return self_energy(both, occupation, shift_offsets, shift_weights)


def solution(mesh):
    placed = (
        P("energy", "space", None, None, None),
        P("space", None, None, None),
        P("energy", "space", None, None, None),
        P("energy", "space", None, None),
        P(),
        P(),
        P(),
    )
    return jax.shard_map(
        body,
        mesh=mesh,
        in_specs=placed,
        out_specs=(P("energy", "space", None, None, None), P("energy", "space", None, None, None)),
        check_vma=False,
    )
```

```python
import functools

import jax
import jax.numpy as jnp
from jax import lax
from jax.experimental import pallas as pl
from jax.experimental.pallas import tpu as pltpu
from jax.sharding import PartitionSpec as P

SWEEPS = 4
MESH = pl.DeviceIdType.MESH
F32 = jnp.float32
BF16 = jnp.bfloat16


def dot(a, b):
    return jnp.dot(a, b, preferred_element_type=F32)


def nt_dot(a, b):
    return lax.dot_general(a, b, (((1,), (1,)), ((), ())), preferred_element_type=F32)


def solve_kernel(n, chunks, pre_hbm, cpl_hbm, src_hbm, sig_ref, out_ref,
                 pre, cpl, src, srcc, st, follow, arrive, hand, other, part,
                 load_sem, send_sem, recv_sem, swap_sem):
    me = lax.axis_index("space")
    en = lax.axis_index("energy")
    prev = lax.rem(me + n - 1, n)
    nxt = lax.rem(me + 1, n)
    mate = 1 - en
    w = st.shape[-2]
    h = w // 2

    loads = [pltpu.make_async_copy(src_hbm.at[0], src, load_sem.at[0])]
    loads += [pltpu.make_async_copy(pre_hbm.at[0, s], pre.at[s], load_sem.at[1 + s]) for s in range(2)]
    loads += [pltpu.make_async_copy(cpl_hbm.at[s], cpl.at[s], load_sem.at[3 + s]) for s in range(2)]
    for c in loads:
        c.start()

    barrier = pltpu.get_barrier_semaphore()
    for peer in ((en, prev), (en, nxt), (mate, me)):
        pl.semaphore_signal(barrier, inc=1, device_id=peer, device_id_type=MESH)

    @pl.when(me == n - 1)
    def _():
        follow[...] = jnp.zeros_like(follow)

    @pl.when(me == 0)
    def _():
        arrive[...] = jnp.zeros_like(arrive)

    def cprod(mr, mi, rhs):
        x = nt_dot(rhs, mr)
        y = nt_dot(rhs, mi)
        return jnp.concatenate([x[:h] - y[h:], x[h:] + y[:h]], axis=0)

    def cprod_adj(mr, mi, rhs):
        x = dot(rhs, mr)
        y = dot(rhs, mi)
        return jnp.concatenate([x[:h] + y[h:], x[h:] - y[:h]], axis=0)

    def local(c, s):
        x = st[c, s].astype(F32)
        xr, xi = x[:h], x[h:]
        gr = sig_ref[0, s, pl.ds(0, 1), :]
        gi = sig_ref[0, s, pl.ds(1, 1), :]
        return srcc[c, s] + jnp.concatenate([gr * xr - gi * xi, gr * xi + gi * xr], axis=0)

    sweeps = SWEEPS - 1

    def sends(sweep, c):
        to_prev = pltpu.make_async_remote_copy(
            src_ref=st.at[c, 0], dst_ref=follow.at[sweep, c],
            send_sem=send_sem.at[0, sweep, c], recv_sem=recv_sem.at[0, sweep, c],
            device_id=(en, prev), device_id_type=MESH)
        to_next = pltpu.make_async_remote_copy(
            src_ref=hand.at[sweep, c], dst_ref=arrive.at[sweep, c],
            send_sem=send_sem.at[1, sweep, c], recv_sem=recv_sem.at[1, sweep, c],
            device_id=(en, nxt), device_id_type=MESH)
        return to_prev, to_next

    copies = [[sends(sweep, c) for c in range(chunks)] for sweep in range(sweeps)]

    loads[0].wait()
    for s in range(2):
        re = src[s, 0].T
        im = src[s, 1].T
        for c in range(chunks):
            srcc[c, s] = jnp.concatenate([re[c * h:(c + 1) * h], im[c * h:(c + 1) * h]], axis=0)

    for s in range(2):
        loads[1 + s].wait()
        rhs = jnp.concatenate([srcc[c, s] for c in range(chunks)], axis=0).astype(BF16)
        x = nt_dot(rhs, pre[s, 0])
        y = nt_dot(rhs, pre[s, 1])
        for c in range(chunks):
            lo, mid, hi = c * w, c * w + h, (c + 1) * w
            st[c, s] = jnp.concatenate(
                [x[lo:mid] - y[mid:hi], x[mid:hi] + y[lo:mid]], axis=0).astype(BF16)
        if s == 0:
            pl.semaphore_wait(barrier, 3)
            for c in range(chunks):
                @pl.when(me > 0)
                def _():
                    copies[0][c][0].start()

    for s in range(2):
        loads[3 + s].wait()

    def phase1(sweep, c):
        to_prev, to_next = copies[sweep][c]
        hand[sweep, c] = cprod_adj(cpl[1, 0], cpl[1, 1], st[c, 1]).astype(BF16)

        @pl.when(me < n - 1)
        def _():
            to_next.start()

        part[c, 2] = cprod_adj(cpl[0, 0], cpl[0, 1], st[c, 0]).astype(BF16).astype(F32)
        part[c, 1] = local(c, 1)
        part[c, 0] = local(c, 0) + cprod(cpl[0, 0], cpl[0, 1], st[c, 1])

    def phase2(sweep, c):
        to_prev, to_next = copies[sweep][c]

        @pl.when(me > 0)
        def _():
            to_next.wait_recv()

        d0 = (part[c, 0] + arrive[sweep, c].astype(F32)).astype(BF16)

        @pl.when(me > 0)
        def _():
            to_prev.wait_send()

        st[c, 0] = cprod(pre[0, 0], pre[0, 1], d0).astype(BF16)
        if sweep + 1 < sweeps:
            @pl.when(me > 0)
            def _():
                copies[sweep + 1][c][0].start()

        @pl.when(me < n - 1)
        def _():
            to_prev.wait_recv()

        upper = cprod(cpl[1, 0], cpl[1, 1], follow[sweep, c])
        d1 = ((part[c, 1] + upper) + part[c, 2]).astype(BF16)
        st[c, 1] = cprod(pre[1, 0], pre[1, 1], d1).astype(BF16)

        @pl.when(me < n - 1)
        def _():
            to_next.wait_send()

    swaps = [pltpu.make_async_remote_copy(
        src_ref=st.at[c], dst_ref=other.at[c], send_sem=swap_sem.at[0, c],
        recv_sem=swap_sem.at[1, c], device_id=(mate, me), device_id_type=MESH)
        for c in range(chunks)]

    for c in range(chunks):
        phase1(0, c)
    for sweep in range(sweeps):
        for c in range(chunks):
            phase2(sweep, c)
            if sweep + 1 < sweeps:
                phase1(sweep + 1, c)
            else:
                swaps[c].start()
                for s in range(2):
                    out_ref[0, s, :, c * w:(c + 1) * w] = st[c, s].T

    for c in range(chunks):
        swaps[c].wait()
        for s in range(2):
            out_ref[1, s, :, c * w:(c + 1) * w] = other[c, s].T


def solve(precond, coupling, source, sigma, n):
    m, h = source.shape[-2:]
    chunks = 2
    sweeps = SWEEPS - 1
    blk = (2 * h // chunks, m)
    vmem = pl.BlockSpec(memory_space=pltpu.VMEM)
    anyspace = pl.BlockSpec(memory_space=pl.ANY)
    return pl.pallas_call(
        functools.partial(solve_kernel, n, chunks),
        out_shape=jax.ShapeDtypeStruct((2, 2, m, 2 * h), BF16),
        in_specs=[anyspace, anyspace, anyspace, vmem],
        out_specs=vmem,
        scratch_shapes=[
            pltpu.VMEM(precond.shape[1:], BF16),
            pltpu.VMEM(coupling.shape, BF16),
            pltpu.VMEM(source.shape[1:], F32),
            pltpu.VMEM((chunks, 2) + blk, F32),
            pltpu.VMEM((chunks, 2) + blk, BF16),
            pltpu.VMEM((sweeps, chunks) + blk, BF16),
            pltpu.VMEM((sweeps, chunks) + blk, BF16),
            pltpu.VMEM((sweeps, chunks) + blk, BF16),
            pltpu.VMEM((chunks, 2) + blk, BF16),
            pltpu.VMEM((chunks, 3) + blk, F32),
            pltpu.SemaphoreType.DMA((5,)),
            pltpu.SemaphoreType.DMA((2, sweeps, chunks)),
            pltpu.SemaphoreType.DMA((2, sweeps, chunks)),
            pltpu.SemaphoreType.DMA((2, chunks)),
        ],
        compiler_params=pltpu.CompilerParams(collective_id=0, has_side_effects=True),
    )(precond, coupling, source, sigma)


def self_kernel(both_ref, occ_ref, off_ref, wt_ref, less_ref, great_ref):
    h = both_ref.shape[-1] // 2
    energy_total = occ_ref.shape[0]
    e = lax.axis_index("energy")
    mate = 1 - e
    coef_own = jnp.float32(0.0)
    coef_mate = jnp.float32(0.0)
    for j in range(off_ref.shape[1]):
        t = e + off_ref[e, j]
        inside = jnp.logical_and(t >= 0, t < energy_total)
        w = jnp.where(inside, wt_ref[e, j], jnp.float32(0.0)) / h
        coef_own = coef_own + jnp.where(t == e, w, jnp.float32(0.0))
        coef_mate = coef_mate + jnp.where(t == mate, w, jnp.float32(0.0))
    occ_own = occ_ref[pl.ds(e, 1), :]
    occ_mate = occ_ref[pl.ds(mate, 1), :]
    lanes = lax.broadcasted_iota(jnp.int32, (1, h), 1)
    low = lanes < h // 2
    pos_low = jnp.where(low, 1.0, -1.0).astype(BF16)

    def turn(x):
        return pltpu.roll(x, h // 2, 1)

    def spread(v):
        return jnp.concatenate([jnp.where(low, v, turn(v)), jnp.where(low, turn(v), v)], axis=1)

    scales = []
    for own_part, mate_part in ((occ_own, occ_mate), (1.0 - occ_own, 1.0 - occ_mate)):
        scales.append(jnp.concatenate([spread(coef_own * own_part), spread(coef_mate * mate_part)], axis=1))
    own = both_ref[0, 0]
    mate_states = both_ref[1, 0]
    a = jnp.concatenate([own, mate_states], axis=1)
    blocks = [x[:, i * h:(i + 1) * h] for x in (own, mate_states) for i in range(2)]
    swapped = jnp.concatenate(
        [(turn(b.astype(F32)) * pos_low.astype(F32)).astype(BF16) for b in blocks], axis=1)
    af = a.astype(F32)
    lhs = jnp.concatenate([a, swapped], axis=0)
    m = a.shape[0]
    for scale, out in zip(scales, (less_ref, great_ref)):
        b = (af * scale).astype(BF16)
        both = nt_dot(lhs, b)
        out[0, 0, 0] = both[:m].astype(BF16)
        out[0, 0, 1] = both[m:].astype(BF16)


def self_energy(both, occupation, shift_offsets, shift_weights):
    m, w = both.shape[2:]
    shape = jax.ShapeDtypeStruct((1, 2, 2, m, m), BF16)
    smem = pl.BlockSpec(memory_space=pltpu.SMEM)
    out_spec = pl.BlockSpec((1, 1, 2, m, m), lambda s: (0, s, 0, 0, 0))
    return pl.pallas_call(
        self_kernel,
        out_shape=(shape, shape),
        grid=(2,),
        in_specs=[
            pl.BlockSpec((2, 1, m, w), lambda s: (0, s, 0, 0)),
            pl.BlockSpec(occupation.shape, lambda s: (0, 0)),
            smem,
            smem,
        ],
        out_specs=(out_spec, out_spec),
    )(both, occupation, shift_offsets, shift_weights)


def body(precond, coupling, source, sigma_ret, occupation, shift_offsets, shift_weights):
    n = lax.axis_size("space")
    both = solve(precond, coupling, source, sigma_ret, n)
    return self_energy(both, occupation, shift_offsets, shift_weights)


def solution(mesh):
    placed = (
        P("energy", "space", None, None, None),
        P("space", None, None, None),
        P("energy", "space", None, None, None),
        P("energy", "space", None, None),
        P(),
        P(),
        P(),
    )
    return jax.shard_map(
        body,
        mesh=mesh,
        in_specs=placed,
        out_specs=(P("energy", "space", None, None, None), P("energy", "space", None, None, None)),
        check_vma=False,
    )
```

```python
import functools

import jax
import jax.numpy as jnp
from jax import lax
from jax.experimental import pallas as pl
from jax.experimental.pallas import tpu as pltpu
from jax.sharding import PartitionSpec as P

SWEEPS = 4
MESH = pl.DeviceIdType.MESH
F32 = jnp.float32
BF16 = jnp.bfloat16


def dot(a, b):
    return jnp.dot(a, b, preferred_element_type=F32)


def nt_dot(a, b):
    return lax.dot_general(a, b, (((1,), (1,)), ((), ())), preferred_element_type=F32)


def solve_kernel(n, chunks, pre_hbm, cpl_hbm, src_hbm, sig_ref, out_ref,
                 pre, cpl, src, srcc, st, follow, arrive, hand, other, part,
                 load_sem, send_sem, recv_sem, swap_sem):
    me = lax.axis_index("space")
    en = lax.axis_index("energy")
    prev = lax.rem(me + n - 1, n)
    nxt = lax.rem(me + 1, n)
    mate = 1 - en
    w = st.shape[-2]
    h = w // 2

    loads = [pltpu.make_async_copy(src_hbm.at[0], src, load_sem.at[0])]
    loads += [pltpu.make_async_copy(pre_hbm.at[0, s], pre.at[s], load_sem.at[1 + s]) for s in range(2)]
    loads += [pltpu.make_async_copy(cpl_hbm.at[s], cpl.at[s], load_sem.at[3 + s]) for s in range(2)]
    for c in loads:
        c.start()

    barrier = pltpu.get_barrier_semaphore()
    for peer in ((en, prev), (en, nxt), (mate, me)):
        pl.semaphore_signal(barrier, inc=1, device_id=peer, device_id_type=MESH)

    @pl.when(me == n - 1)
    def _():
        follow[...] = jnp.zeros_like(follow)

    @pl.when(me == 0)
    def _():
        arrive[...] = jnp.zeros_like(arrive)

    def cprod(mr, mi, rhs):
        x = nt_dot(rhs, mr)
        y = nt_dot(rhs, mi)
        return jnp.concatenate([x[:h] - y[h:], x[h:] + y[:h]], axis=0)

    def cprod_adj(mr, mi, rhs):
        x = dot(rhs, mr)
        y = dot(rhs, mi)
        return jnp.concatenate([x[:h] + y[h:], x[h:] - y[:h]], axis=0)

    def local(c, s):
        x = st[c, s].astype(F32)
        xr, xi = x[:h], x[h:]
        gr = sig_ref[0, s, pl.ds(0, 1), :]
        gi = sig_ref[0, s, pl.ds(1, 1), :]
        return srcc[c, s] + jnp.concatenate([gr * xr - gi * xi, gr * xi + gi * xr], axis=0)

    sweeps = SWEEPS - 1

    def sends(sweep, c):
        to_prev = pltpu.make_async_remote_copy(
            src_ref=st.at[c, 0], dst_ref=follow.at[sweep, c],
            send_sem=send_sem.at[0, sweep, c], recv_sem=recv_sem.at[0, sweep, c],
            device_id=(en, prev), device_id_type=MESH)
        to_next = pltpu.make_async_remote_copy(
            src_ref=hand.at[sweep, c], dst_ref=arrive.at[sweep, c],
            send_sem=send_sem.at[1, sweep, c], recv_sem=recv_sem.at[1, sweep, c],
            device_id=(en, nxt), device_id_type=MESH)
        return to_prev, to_next

    copies = [[sends(sweep, c) for c in range(chunks)] for sweep in range(sweeps)]

    loads[0].wait()
    for s in range(2):
        re = src[s, 0].T
        im = src[s, 1].T
        for c in range(chunks):
            srcc[c, s] = jnp.concatenate([re[c * h:(c + 1) * h], im[c * h:(c + 1) * h]], axis=0)

    for s in range(2):
        loads[1 + s].wait()
        rhs = jnp.concatenate([srcc[c, s] for c in range(chunks)], axis=0).astype(BF16)
        x = nt_dot(rhs, pre[s, 0])
        y = nt_dot(rhs, pre[s, 1])
        for c in range(chunks):
            lo, mid, hi = c * w, c * w + h, (c + 1) * w
            st[c, s] = jnp.concatenate(
                [x[lo:mid] - y[mid:hi], x[mid:hi] + y[lo:mid]], axis=0).astype(BF16)

    pl.semaphore_wait(barrier, 3)
    for c in range(chunks):
        @pl.when(me > 0)
        def _():
            copies[0][c][0].start()

    for s in range(2):
        loads[3 + s].wait()

    def phase1(sweep, c):
        to_prev, to_next = copies[sweep][c]
        hand[sweep, c] = cprod_adj(cpl[1, 0], cpl[1, 1], st[c, 1]).astype(BF16)

        @pl.when(me < n - 1)
        def _():
            to_next.start()

        part[c, 2] = cprod_adj(cpl[0, 0], cpl[0, 1], st[c, 0]).astype(BF16).astype(F32)
        part[c, 1] = local(c, 1)
        part[c, 0] = local(c, 0) + cprod(cpl[0, 0], cpl[0, 1], st[c, 1])

    def phase2(sweep, c):
        to_prev, to_next = copies[sweep][c]

        @pl.when(me > 0)
        def _():
            to_next.wait_recv()

        d0 = (part[c, 0] + arrive[sweep, c].astype(F32)).astype(BF16)

        @pl.when(me > 0)
        def _():
            to_prev.wait_send()

        st[c, 0] = cprod(pre[0, 0], pre[0, 1], d0).astype(BF16)
        if sweep + 1 < sweeps:
            @pl.when(me > 0)
            def _():
                copies[sweep + 1][c][0].start()

        @pl.when(me < n - 1)
        def _():
            to_prev.wait_recv()

        upper = cprod(cpl[1, 0], cpl[1, 1], follow[sweep, c])
        d1 = ((part[c, 1] + upper) + part[c, 2]).astype(BF16)
        st[c, 1] = cprod(pre[1, 0], pre[1, 1], d1).astype(BF16)

        @pl.when(me < n - 1)
        def _():
            to_next.wait_send()

    swaps = [pltpu.make_async_remote_copy(
        src_ref=st.at[c], dst_ref=other.at[c], send_sem=swap_sem.at[0, c],
        recv_sem=swap_sem.at[1, c], device_id=(mate, me), device_id_type=MESH)
        for c in range(chunks)]

    for c in range(chunks):
        phase1(0, c)
    for sweep in range(sweeps):
        for c in range(chunks):
            phase2(sweep, c)
            if sweep + 1 < sweeps:
                phase1(sweep + 1, c)
            else:
                swaps[c].start()
                for s in range(2):
                    out_ref[0, s, :, c * w:(c + 1) * w] = st[c, s].T

    for c in range(chunks):
        swaps[c].wait()
        for s in range(2):
            out_ref[1, s, :, c * w:(c + 1) * w] = other[c, s].T


def solve(precond, coupling, source, sigma, n):
    m, h = source.shape[-2:]
    chunks = 2
    sweeps = SWEEPS - 1
    blk = (2 * h // chunks, m)
    vmem = pl.BlockSpec(memory_space=pltpu.VMEM)
    anyspace = pl.BlockSpec(memory_space=pl.ANY)
    return pl.pallas_call(
        functools.partial(solve_kernel, n, chunks),
        out_shape=jax.ShapeDtypeStruct((2, 2, m, 2 * h), BF16),
        in_specs=[anyspace, anyspace, anyspace, vmem],
        out_specs=vmem,
        scratch_shapes=[
            pltpu.VMEM(precond.shape[1:], BF16),
            pltpu.VMEM(coupling.shape, BF16),
            pltpu.VMEM(source.shape[1:], F32),
            pltpu.VMEM((chunks, 2) + blk, F32),
            pltpu.VMEM((chunks, 2) + blk, BF16),
            pltpu.VMEM((sweeps, chunks) + blk, BF16),
            pltpu.VMEM((sweeps, chunks) + blk, BF16),
            pltpu.VMEM((sweeps, chunks) + blk, BF16),
            pltpu.VMEM((chunks, 2) + blk, BF16),
            pltpu.VMEM((chunks, 3) + blk, F32),
            pltpu.SemaphoreType.DMA((5,)),
            pltpu.SemaphoreType.DMA((2, sweeps, chunks)),
            pltpu.SemaphoreType.DMA((2, sweeps, chunks)),
            pltpu.SemaphoreType.DMA((2, chunks)),
        ],
        compiler_params=pltpu.CompilerParams(collective_id=0, has_side_effects=True),
    )(precond, coupling, source, sigma)


def self_kernel(both_ref, occ_ref, off_ref, wt_ref, less_ref, great_ref):
    h = both_ref.shape[-1] // 2
    energy_total = occ_ref.shape[0]
    e = lax.axis_index("energy")
    mate = 1 - e
    coef_own = jnp.float32(0.0)
    coef_mate = jnp.float32(0.0)
    for j in range(off_ref.shape[1]):
        t = e + off_ref[e, j]
        inside = jnp.logical_and(t >= 0, t < energy_total)
        w = jnp.where(inside, wt_ref[e, j], jnp.float32(0.0)) / h
        coef_own = coef_own + jnp.where(t == e, w, jnp.float32(0.0))
        coef_mate = coef_mate + jnp.where(t == mate, w, jnp.float32(0.0))
    occ_own = occ_ref[pl.ds(e, 1), :]
    occ_mate = occ_ref[pl.ds(mate, 1), :]
    lanes = lax.broadcasted_iota(jnp.int32, (1, h), 1)
    low = lanes < h // 2
    pos_low = jnp.where(low, 1.0, -1.0).astype(BF16)

    def turn(x):
        return pltpu.roll(x, h // 2, 1)

    def spread(v):
        return jnp.concatenate([jnp.where(low, v, turn(v)), jnp.where(low, turn(v), v)], axis=1)

    scales = []
    for own_part, mate_part in ((occ_own, occ_mate), (1.0 - occ_own, 1.0 - occ_mate)):
        scales.append(jnp.concatenate([spread(coef_own * own_part), spread(coef_mate * mate_part)], axis=1))
    own = both_ref[0, 0]
    mate_states = both_ref[1, 0]
    a = jnp.concatenate([own, mate_states], axis=1)
    blocks = [x[:, i * h:(i + 1) * h] for x in (own, mate_states) for i in range(2)]
    swapped = jnp.concatenate(
        [(turn(b.astype(F32)) * pos_low.astype(F32)).astype(BF16) for b in blocks], axis=1)
    af = a.astype(F32)
    lhs = jnp.concatenate([a, swapped], axis=0)
    m = a.shape[0]
    for scale, out in zip(scales, (less_ref, great_ref)):
        b = (af * scale).astype(BF16)
        both = nt_dot(lhs, b)
        out[0, 0, 0] = both[:m].astype(BF16)
        out[0, 0, 1] = both[m:].astype(BF16)


def self_energy(both, occupation, shift_offsets, shift_weights):
    m, w = both.shape[2:]
    shape = jax.ShapeDtypeStruct((1, 2, 2, m, m), BF16)
    smem = pl.BlockSpec(memory_space=pltpu.SMEM)
    out_spec = pl.BlockSpec((1, 1, 2, m, m), lambda s: (0, s, 0, 0, 0))
    return pl.pallas_call(
        self_kernel,
        out_shape=(shape, shape),
        grid=(2,),
        in_specs=[
            pl.BlockSpec((2, 1, m, w), lambda s: (0, s, 0, 0)),
            pl.BlockSpec(occupation.shape, lambda s: (0, 0)),
            smem,
            smem,
        ],
        out_specs=(out_spec, out_spec),
    )(both, occupation, shift_offsets, shift_weights)


def body(precond, coupling, source, sigma_ret, occupation, shift_offsets, shift_weights):
    n = lax.axis_size("space")
    both = solve(precond, coupling, source, sigma_ret, n)
    return self_energy(both, occupation, shift_offsets, shift_weights)


def solution(mesh):
    placed = (
        P("energy", "space", None, None, None),
        P("space", None, None, None),
        P("energy", "space", None, None, None),
        P("energy", "space", None, None),
        P(),
        P(),
        P(),
    )
    return jax.shard_map(
        body,
        mesh=mesh,
        in_specs=placed,
        out_specs=(P("energy", "space", None, None, None), P("energy", "space", None, None, None)),
        check_vma=False,
    )
```
